32 devices in a mesh: layer: 8 (over z, x), row: 4 (over y, core).
Axes of the slice: x: 2, y: 2, z: 4, core: 2. Of those that a mesh axis runs over, the one named last changes fastest.
Arguments:
- leaf_rhs: bfloat16 [32768, 512], P(('layer', 'row')), may hold values from -3 to 3
- leaf_inv: bfloat16 [256, 128, 128], P(('layer', 'row')), may hold values from -1 to 1.25, as said below
- coupling: bfloat16 [32768, 3, 256], P(('layer', 'row')), may hold values from -0.09375 to 0.09375
- pattern: int32 [256, 3], P(('layer', 'row')), may hold values 0 or 1
- anc_rhs: float32 [8, 3, 1024, 512], P('layer', None, 'row'), may hold values from -2 to 2
- anc_blocks: bfloat16 [8, 6, 1024, 1024], P('layer', None, 'row'), may hold values from -1 to 1.25, as said below
Outputs:
- x_leaf: float32 [32768, 512], P(('layer', 'row'))
- x_anc: float32 [8, 3, 1024, 512], P('layer', None, 'row')
The draws below stay inside these ranges and needn't reach their ends.
Inputs may be any that keep to these rules, and one draw needn't show every extreme that they name: `leaf_inv`: each block is lower triangular with a positive diagonal. For every level t and block index k of blk(s, t), the copies anc_blocks[l, k] are equal for all layers l of one group of 2 ** (t + 1) layers; the blocks blk(t, t) are lower triangular with a positive diagonal.
All inputs are finite; a program needn't handle non-finite values. No bound on the sum of `pattern` on one device may be relied on, other than what follows from the above.
Results may differ from the reference program's by a relative error of at most 0.009.
Values may be sent and summed in bfloat16 or wider, within the bound.
A program may use at most 64 MiB of HBM per device.

```python
import math
import jax
import jax.numpy as jnp
from jax import lax

B = 128
R = 512
ANC = 1024
SN_DEV = 8
LEVELS = 3
ANC_DEV = 256
LEAF_SN = 256
LEAF_ROWS = 32768
N_LAYER = 8
N_ROW = 4


def lower_inverse(key, block_count, block_order):
    key_diagonal, key_lower = jax.random.split(key)
    row_ids = jnp.arange(block_order)[:, None]
    column_ids = jnp.arange(block_order)[None, :]
    below_mask = (row_ids > column_ids).astype(jnp.float32)
    diagonal_part = jax.random.uniform(key_diagonal, (block_count, block_order), jnp.float32, 0.6, 1.2)
    lower_part = jnp.clip(jax.random.normal(key_lower, (block_count, block_order, block_order), jnp.float32), -4.0, 4.0)
    lower_part = lower_part * (0.5 / math.sqrt(block_order * 1.0)) * below_mask
    return lower_part + diagonal_part[:, :, None] * jnp.eye(block_order, dtype=jnp.float32)


def draw_leaf_inv(key, part):
    return lower_inverse(jax.random.fold_in(key, 11), LEAF_SN, B).astype(jnp.bfloat16)


def draw_anc_blocks(key, part):
    layer_total = 2 ** LEVELS
    blocks_out = []
    for tree_level in range(LEVELS):
        group_size = 2 ** (tree_level + 1)
        group_count = layer_total // group_size
        for above in range(tree_level, LEVELS):
            sub_key = jax.random.fold_in(jax.random.fold_in(key, 31 + tree_level), above)
            if above == tree_level:
                fresh = lower_inverse(sub_key, group_count, ANC)
            else:
                scale_value = 0.6 / math.sqrt(ANC * 2.0 ** (above - tree_level))
                fresh = jnp.clip(jax.random.normal(sub_key, (group_count, ANC, ANC), jnp.float32), -4.0, 4.0) * scale_value
            blocks_out.append(jnp.repeat(fresh.astype(jnp.bfloat16), group_size, axis=0))
    return jnp.stack(blocks_out, axis=1)


def draw_anc_rhs(key, part):
    sub_key = jax.random.fold_in(key, 57)
    shape_full = (2 ** LEVELS, LEVELS, ANC, R)
    scales = 0.5 * 2.0 ** (-(jnp.arange(LEVELS, dtype=jnp.float32) + 1.0) / 2.0)
    base_values = jnp.clip(jax.random.normal(sub_key, shape_full, jnp.float32), -4.0, 4.0)
    return base_values * scales[None, :, None, None]


def touch_ends(result, own_key, low, high):
    extent = result.shape
    spot = [jax.random.randint(jax.random.fold_in(own_key, axis), (), 0, extent[axis]) for axis in range(len(extent))]
    result = result.at[tuple(spot)].set(low)
    longest = extent.index(max(extent))
    spot[longest] = (spot[longest] + 1) % extent[longest]
    return result.at[tuple(spot)].set(high)


def block_levels(key, shape, shards, smallest, largest):
    loudness, own = 1.0, jax.random.fold_in(key, 6)
    for axis_at, parts in shards:
        heights = jnp.exp(jax.random.uniform(jax.random.fold_in(own, axis_at), (parts,), jnp.float32, smallest / len(shards), largest / len(shards)))
        loudness = loudness * jnp.repeat(heights, shape[axis_at] // parts).reshape([-1 if axis == axis_at else 1 for axis in range(len(shape))])
    return loudness


def scatter_about(own_key, extent, deviation, most, shards=(), kind=jnp.bfloat16):
    entries = deviation * jax.random.normal(own_key, extent, jnp.float32)
    if shards:
        entries = entries * block_levels(own_key, extent, shards, -0.22, 0.18)
    return jnp.clip(entries, -most, most).astype(kind)


def setup_inputs(seed: int = 0) -> dict:
    key_of = jax.random.split(jax.random.key(seed), 7)
    leaf_rhs = scatter_about(key_of[0], (LEAF_ROWS, R), 0.5, 3.0, ((0, 32),))
    leaf_inv = draw_leaf_inv(jax.random.fold_in(key_of[6], 71), 0)
    coupling = scatter_about(key_of[2], (LEAF_ROWS, LEVELS, ANC_DEV), (SN_DEV * B * N_LAYER // 2) ** -0.5, 0.09375, ((0, 32),))
    pattern = touch_ends((jax.random.randint(key_of[3], (LEAF_SN, LEVELS), 0, 4) < 3).astype(jnp.int32), jax.random.fold_in(key_of[3], 1), 0, 1)
    anc_rhs = draw_anc_rhs(jax.random.fold_in(key_of[6], 71), 0)
    anc_blocks = draw_anc_blocks(jax.random.fold_in(key_of[6], 71), 0)
    return dict(leaf_rhs=leaf_rhs, leaf_inv=leaf_inv, coupling=coupling, pattern=pattern, anc_rhs=anc_rhs, anc_blocks=anc_blocks)


def block_start(tree_level, level_total):
    return tree_level * level_total - tree_level * (tree_level - 1) // 2


def reference(leaf_rhs, leaf_inv, coupling, pattern, anc_rhs, anc_blocks):
    devices = N_LAYER * N_ROW
    rows_dev = SN_DEV * B
    right_dev = leaf_rhs.reshape(devices, SN_DEV, B, R)
    inverse_dev = leaf_inv.reshape(devices, SN_DEV, B, B)
    coupling_dev = coupling.reshape(devices, SN_DEV, B, LEVELS, ANC_DEV)
    pattern_dev = pattern.reshape(devices, SN_DEV, LEVELS)

    def masked_of(coupling_one, pattern_one):
        scaled = coupling_one * pattern_one.astype(jnp.bfloat16)[:, None, :, None]
        return scaled.reshape(rows_dev, LEVELS * ANC_DEV)

    def forward_leaf(operands):
        right_side, inverse, coupling_one, pattern_one = operands
        leaf_y = jnp.einsum("kab,kbr->kar", inverse.astype(jnp.float32), right_side.astype(jnp.float32))
        leaf_yb = leaf_y.astype(jnp.bfloat16).reshape(rows_dev, R)
        masked = masked_of(coupling_one, pattern_one)
        leaf_terms = jnp.dot(masked.T, leaf_yb, preferred_element_type=jnp.float32)
        return leaf_y, leaf_terms.reshape(LEVELS, ANC_DEV, R)

    leaf_y, leaf_terms = lax.map(forward_leaf, (right_dev, inverse_dev, coupling_dev, pattern_dev))
    leaf_terms = leaf_terms.reshape(N_LAYER, N_ROW, LEVELS, ANC_DEV, R)
    leaf_terms = leaf_terms.transpose(0, 2, 1, 3, 4).reshape(N_LAYER, LEVELS, ANC, R)
    share = anc_rhs - leaf_terms
    lowered = jnp.zeros((N_LAYER, LEVELS, ANC, R), jnp.float32)
    y_list = []
    for tree_level in range(LEVELS):
        group_size = 2 ** (tree_level + 1)
        group_count = N_LAYER // group_size
        level_total = (share[:, tree_level] - lowered[:, tree_level]).reshape(group_count, group_size, ANC, R).sum(axis=1)
        z_level = level_total.astype(jnp.bfloat16)
        first_block = block_start(tree_level, LEVELS)
        blocks = anc_blocks[::group_size, first_block:first_block + LEVELS - tree_level].astype(jnp.float32)
        product = jnp.einsum("gkab,gbr->gkar", blocks, z_level.astype(jnp.float32))
        y_list.append(product[:, 0].astype(jnp.bfloat16))
        for above in range(tree_level + 1, LEVELS):
            lowered = lowered.at[::group_size, above].add(product[:, above - tree_level])
    answers = [None] * LEVELS
    for tree_level in reversed(range(LEVELS)):
        group_size = 2 ** (tree_level + 1)
        first_block = block_start(tree_level, LEVELS)
        blocks = anc_blocks[::group_size, first_block:first_block + LEVELS - tree_level].astype(jnp.float32)
        pieces_list = [y_list[tree_level]]
        for above in range(tree_level + 1, LEVELS):
            pieces_list.append(-jnp.repeat(answers[above].astype(jnp.bfloat16), 2 ** (above - tree_level), axis=0))
        stacked_vals = jnp.stack(pieces_list, axis=1).astype(jnp.float32)
        answers[tree_level] = jnp.einsum("gkab,gkar->gbr", blocks, stacked_vals)
    x_anc = jnp.stack([jnp.repeat(answers[tree_level], 2 ** (tree_level + 1), axis=0) for tree_level in range(LEVELS)], axis=1)
    solved_bf = x_anc.astype(jnp.bfloat16).reshape(N_LAYER, LEVELS, N_ROW, ANC_DEV, R)
    solved_bf = solved_bf.transpose(0, 2, 1, 3, 4).reshape(devices, LEVELS * ANC_DEV, R)

    def backward_leaf(operands):
        leaf_one, inverse, coupling_one, pattern_one, solved_one = operands
        masked = masked_of(coupling_one, pattern_one)
        back_terms = jnp.dot(masked, solved_one, preferred_element_type=jnp.float32)
        leaf_vb = (leaf_one.reshape(rows_dev, R) - back_terms).astype(jnp.bfloat16)
        return jnp.einsum("kba,kbr->kar", inverse.astype(jnp.float32), leaf_vb.reshape(SN_DEV, B, R).astype(jnp.float32))

    x_leaf = lax.map(backward_leaf, (leaf_y, inverse_dev, coupling_dev, pattern_dev, solved_bf))
    return x_leaf.reshape(LEAF_ROWS, R), x_anc
```

```python
import functools

import jax
import jax.numpy as jnp
from jax import lax
from jax.experimental import pallas as pl
from jax.experimental.pallas import tpu as pltpu
from jax.sharding import PartitionSpec as P

MESH = pl.DeviceIdType.MESH
LANES = 128
VMEM_BYTES = 56 * 2**20
BF, F32 = jnp.bfloat16, jnp.float32


def block_start(tree_level, level_total):
    return tree_level * level_total - tree_level * (tree_level - 1) // 2


def plan(levels, cols):
    counts, splits, count = [], [], cols // LANES
    for _ in range(levels):
        split = count % 2 == 0
        count = count // 2 if split else count
        counts.append(count)
        splits.append(split)
    return counts, splits


def tdot(a, b):
    return lax.dot_general(a, b, (((0,), (0,)), ((), ())), preferred_element_type=F32)


def dot(a, b):
    return jnp.dot(a, b, preferred_element_type=F32)


def dot_t(a, b):
    return lax.dot_general(a, b, (((1,), (1,)), ((), ())), preferred_element_type=F32)


class Copies:
    def __init__(self, send, recv):
        self.send, self.recv, self.count, self.all = send, recv, 0, []

    def start(self, src, dst, device):
        copy = pltpu.make_async_remote_copy(
            src_ref=src,
            dst_ref=dst,
            send_sem=self.send.at[self.count],
            recv_sem=self.recv.at[self.count],
            device_id=device,
            device_id_type=MESH,
        )
        copy.start()
        self.count += 1
        self.all.append(copy)
        return copy


def copies_needed(levels, n_row, counts):
    half = n_row // 2
    total = 2 * (1 + 8 * (half - 1)) + 8 * n_row + 2 * half
    for t in range(levels - 2):
        total += counts[t] * (2 * (levels - t) + 1 + 2 * (half - 1) + half + half - 1)
    return total


def kernel(dims, rhs_in, inv_in, coup_in, pat, ancr_in, anc_in, leaf_out, out, *scratch):
    levels, n_row, blocks, supers, width = dims
    rhs, inv, coup, ancr, anc, ly, yb, mk, mt, atr, pend, wide = scratch[:12]
    full, pair, xt, zr, kt, tt, rt, st, wr, zx, yx, pf, px, qx = scratch[12:26]
    used = 26
    mid, top = levels - 2, levels - 1
    groups = []
    for _ in range(8):
        groups.append(scratch[used : used + mid])
        used += mid
    tx, rx, zs, acc, ps, pr, qs, qr = groups
    send, recv, local = scratch[used:]
    counts, splits = plan(levels, blocks * LANES)
    rows = anc.shape[1]
    half = n_row // 2
    strip = LANES // n_row
    early = block_start(mid, levels)
    lay = lax.axis_index("layer")
    row = lax.axis_index("row")
    core = lax.rem(row, 2)
    yy = row // 2
    mate = {"row": yy * 2 + (1 - core)}
    bits = [lax.rem(lay // 2**t, 2) for t in range(levels)]
    across = [{"layer": lay + (1 - 2 * bits[t]) * 2**t} for t in range(levels)]

    def slab(r, part=0, parts=1):
        size = rows // parts
        return pl.ds(pl.multiple_of(r * rows + part * size, size), size)

    loads = {}

    def load(name, src, dst):
        loads[name] = pltpu.make_async_copy(src, dst, local.at[len(loads)])
        loads[name].start()

    load("rhs", rhs_in, rhs)
    load("inv", inv_in, inv)
    load("cross", anc_in.at[early + 1], full.at[0, slab(row)])
    for s in range(levels):
        load(("coup", s), coup_in.at[s], coup.at[s])
        load(("ancr", s), ancr_in.at[s], ancr.at[s])
    load("top", anc_in.at[early + 2], full.at[1, slab(row)])
    load("anc", anc_in.at[pl.ds(0, early)], anc)
    load("mid", anc_in.at[early], pair.at[slab(core)])

    barrier = pltpu.get_barrier_semaphore()
    peers = [{"row": lax.rem(row + i, n_row)} for i in range(n_row)]
    friends = [{**across[mid], **peer} for peer in peers]
    greet = peers[1:] + friends[1:] + across
    for other in greet:
        pl.semaphore_signal(barrier, inc=1, device_id=other, device_id_type=MESH)
    copies = Copies(send, recv)

    spread = {}
    way = [mid, 0]

    def sender(i):
        return lax.rem(yy - i + half, half) * 2 + core

    def push(key, k, where, device):
        spot = full.at[k, where]
        spread[key] = copies.start(spot, spot, device)

    def piece_of(r, k, q, mine):
        h = bits[way[k]] if mine else 1 - bits[way[k]]
        return slab(r, 2 * h + q, 4)

    def spread_first(k, q):
        def push_own(key, where_from, where_to, device):
            spread[key] = copies.start(
                anc_in.at[early + 1 + k, where_from], full.at[k, where_to], device
            )

        h = bits[way[k]]
        size = rows // 4
        src = pl.ds(pl.multiple_of((2 * h + q) * size, size), size)
        for i in range(1, half):
            other = {"row": lax.rem(yy + i, half) * 2 + core}
            push_own((k, q, "y", i), src, piece_of(row, k, q, True), other)
        if q == 0:
            push_own((k, "own"), pl.ds(0, rows), slab(row), mate)

    def spread_next(k, q):
        for i in range(1, half):
            spread[k, q, "y", i].wait_recv()
            where = piece_of(sender(i), k, q, True)
            push((k, q, "far", i), k, where, across[way[k]])
            push((k, q, "mate", i), k, where, mate)

    def spread_last(k, q):
        for i in range(1, half):
            spread[k, q, "far", i].wait_recv()
            push((k, q, "mate2", i), k, piece_of(sender(i), k, q, False), mate)

    def spread_done(k):
        spread[k, "own"].wait_recv()
        for q in range(2):
            for i in range(1, half):
                spread[k, q, "mate", i].wait_recv()
                spread[k, q, "mate2", i].wait_recv()

    order = list(range(counts[-1]))
    for t in reversed(range(levels)):
        if splits[t]:
            near = [bits[t] * counts[t] + j for j in order]
            order = [(1 - bits[t]) * counts[t] + j for j in order] + near
    columns = [pl.ds(pl.multiple_of(j * LANES, LANES), LANES) for j in order]

    def own(t):
        return list(range(blocks - counts[t], blocks))

    def theirs(t, p):
        return p - counts[t] if splits[t] else p

    pl.semaphore_wait(barrier, len(greet))
    spread_first(0, 0)
    spread_first(0, 1)
    spread_first(1, 0)
    halves = copies.start(anc_in.at[early], pair.at[slab(core)], mate)
    loads["rhs"].wait()
    loads["inv"].wait()
    for k in range(supers):
        part = slice(k * width, (k + 1) * width)
        value = dot(inv[k], rhs[part])
        ly[part] = value
        yb[part] = value.astype(BF)

    def mask(s):
        loads["coup", s].wait()
        cut = slice(s * rows, (s + 1) * rows)
        for k in range(supers):
            part = slice(k * width, (k + 1) * width)
            value = coup[s, part].astype(F32) * pat[s, k].astype(F32)
            mk[part, cut] = value.astype(BF)
            mt[s, :, part] = value.T.astype(BF)

    def share(s, where):
        if ("ancr", s) in loads:
            loads.pop(("ancr", s)).wait()
        for first in range(0, len(where), 2):
            two = where[first : first + 2]
            value = dot(mt[s], jnp.concatenate([yb[:, columns[p]] for p in two], axis=1))
            for n, p in enumerate(two):
                yield ancr[s, :, columns[p]] - value[:, n * LANES : (n + 1) * LANES]

    flight = {}

    def offer_urgent(t, p, value):
        n = p - (blocks - counts[t])
        tx[t][n, 0] = value.astype(BF)
        one = pl.ds(0, 1)
        flight[t, p, 0] = copies.start(tx[t].at[n, one], rx[t].at[n, one], across[t])

    def offer_rest(t, p, values):
        n = p - (blocks - counts[t])
        for k, value in enumerate(values):
            tx[t][n, 1 + k] = value.astype(BF)
            one = pl.ds(1 + k, 1)
            flight[t, p, 1 + k] = copies.start(tx[t].at[n, one], rx[t].at[n, one], across[t])

    mask(0)
    mine = own(0)
    away = [theirs(0, p) for p in mine]
    first_shares = list(share(0, away))
    for p, value in zip(mine, first_shares):
        offer_urgent(0, p, value)
    for p, value in zip(mine, share(0, mine)):
        pend[0, p] = value
    for s in range(1, levels):
        mask(s)
    later_shares = [list(share(s, away)) for s in range(1, levels)]
    for n, p in enumerate(mine):
        offer_rest(0, p, [values[n] for values in later_shares])
    for s in range(1, levels):
        for p, value in zip(mine, share(s, mine)):
            pend[s, p] = value
    loads["anc"].wait()
    spread_next(0, 0)

    def turn(k):
        for other in range(n_row):
            cut = slice(other * rows, (other + 1) * rows)
            atr[k, cut] = anc[k, :, cut].T

    kept_block = own(mid)[0]
    given_block = theirs(mid, kept_block)
    near, far = {}, {}

    def hand_over(j, p):
        b = 0 if p == kept_block else 1
        xt[b, j] = pend[mid + j, p].T.astype(BF)

        def piece(i):
            return xt.at[b, j, pl.ds(pl.multiple_of(peers[i]["row"] * strip, strip), strip)]

        if p == given_block:
            for i in range(n_row):
                far[j, i] = copies.start(piece(i), zr.at[1, j, :, slab(row)], friends[i])
        if p == kept_block:
            for i in range(1, n_row):
                near[j, i] = copies.start(piece(i), zr.at[0, j, :, slab(row)], peers[i])
            zr[0, j, :, slab(row)] = piece(0)[...]

    later_work = None
    for t in range(mid):
        first_block = block_start(t, levels)
        above = levels - t - 1
        if later_work is not None:
            later_work()
        gathers, to_mate = {}, {}
        for p in own(t):
            n = p - (blocks - counts[t])
            flight[t, p, 0].wait_recv()
            zs[t][n, row] = (pend[t, p] + rx[t][n, 0].astype(F32)).astype(BF)
            spot = zs[t].at[n, row]
            for i in range(1, half):
                other = lax.rem(yy + i, half) * 2 + core
                gathers[p, i] = copies.start(spot, spot, {"row": other})
            to_mate[p] = copies.start(spot, spot, mate)
        for s in range(t + 1, levels):
            turn(first_block + s - t)
        if t == 0:
            spread_next(0, 1)
            spread_first(1, 1)
        for p in own(t):
            n = p - (blocks - counts[t])

            def sums_of(slot, n=n):
                cut = pl.ds(pl.multiple_of(slot * rows, LANES), rows)
                return [
                    dot(anc[first_block + k, :, cut], zs[t][n, slot]) for k in range(1, above + 1)
                ]

            def add(old, new):
                return [a + b for a, b in zip(old, new)]

            if t == 0 and p == own(t)[-1]:
                spread_next(1, 0)
            total = sums_of(row)
            to_mate[p].wait_recv()
            total = add(total, sums_of(yy * 2 + 1 - core))
            passed = {}
            for i in range(1, half):
                gathers[p, i].wait_recv()
                origin = lax.rem(yy - i + half, half) * 2
                spot = zs[t].at[n, origin + core]
                passed[i] = copies.start(spot, spot, mate)
                total = add(total, sums_of(origin + core))
            for i in range(1, half):
                passed[i].wait_recv()
                origin = lax.rem(yy - i + half, half) * 2
                total = add(total, sums_of(origin + 1 - core))
            for k in range(above):
                flight[t, p, 1 + k].wait_recv()
                pend[t + 1 + k, p] = pend[t + 1 + k, p] + rx[t][n, 1 + k].astype(F32) - total[k]
                if t + 1 == mid:
                    hand_over(k, p)
            if t + 1 < mid:
                for q in own(t + 1):
                    if theirs(t + 1, q) == p:
                        offer_urgent(t + 1, q, pend[t + 1, p])
                        offer_rest(t + 1, q, [pend[s, p] for s in range(t + 2, levels)])

        def later_work(t=t, first_block=first_block):
            z_all = jnp.concatenate(
                [zs[t][n].reshape(n_row * rows, LANES) for n in range(counts[t])], axis=1
            )
            y_here = dot(anc[first_block], z_all).astype(BF)
            for other in range(n_row):
                acc[t][other] = tdot(anc[first_block, :, other * rows : (other + 1) * rows], y_here)

    later_work()
    spread_last(0, 0)
    spread_last(0, 1)
    for name in ("cross", "top", "mid"):
        loads[name].wait()
    halves.wait_recv()
    spread_next(1, 1)

    def gathered(j):
        for i in range(1, n_row):
            near[j, i].wait_recv()
        for i in range(n_row):
            far[j, i].wait_recv()
        return zr[0, j].astype(F32) + zr[1, j].astype(F32)

    z_mid = gathered(0).astype(BF)
    zx[yy] = z_mid
    asked = [
        copies.start(zx.at[yy], zx.at[yy], {"row": lax.rem(yy + i, half) * 2 + core})
        for i in range(1, half)
    ]
    spread_done(0)
    kt[...] = gathered(1) - dot_t(z_mid, full[0])
    tt[...] = kt[...].astype(BF)
    last = copies.start(tt, rt, across[top])
    spread_last(1, 0)
    spread_last(1, 1)
    for copy in asked:
        copy.wait_recv()
    tall = n_row * rows
    yx[...] = dot_t(zx[...].reshape(half * strip, tall), pair[...]).astype(BF)
    pf[...] = dot(yx[...], pair[...]).reshape(half, strip, tall)
    px[...] = pf[...].astype(BF)
    told = []
    for i in range(1, half):
        other = lax.rem(yy + i, half)
        told.append(copies.start(px.at[other], qx.at[yy], {"row": other * 2 + core}))
    spread_done(1)
    last.wait_recv()
    z_top = (kt[...] + rt[...].astype(F32)).astype(BF)
    y_top = dot_t(z_top, full[1]).astype(BF)
    back = {}

    def give_back(j):
        here = pl.ds(pl.multiple_of(row * strip, strip), strip)
        sides = [peers, friends] if splits[mid] else [peers]
        for side, group in enumerate(sides):
            for i in range(1 - side, n_row):
                part = st.at[j, :, slab(peers[i]["row"])]
                back[j, side, i] = copies.start(part, wr.at[j, side, here], group[i])
        wr[j, 0, here] = st[j, :, slab(row)]

    def take_back(j):
        for side, p in ((0, kept_block), (1, given_block)):
            if side == 0 or splits[mid]:
                for i in range(1 - side, n_row):
                    back[j, side, i].wait_recv()
                wide[mid + j, p] = wr[j, side].T

    st[1] = dot(y_top, full[1]).astype(BF)
    give_back(1)
    value = pf[yy] - dot(st[1], full[0])
    for copy in told:
        copy.wait_recv()
    for i in range(1, half):
        value = value + qx[lax.rem(yy + i, half)].astype(F32)
    st[0] = value.astype(BF)
    give_back(0)
    take_back(1)
    take_back(0)

    arriving = {}

    def need(s, p):
        copy = arriving.pop((s, p), None)
        if copy is not None:
            copy.wait_recv()

    def widen(s, p, t):
        if splits[t]:
            arriving[s, p - counts[t]] = copies.start(
                wide.at[s, p], wide.at[s, p - counts[t]], across[t]
            )

    def leaf_back(first, last, p):
        terms = jnp.concatenate([wide[s, p] for s in range(first, last)], axis=0)
        return ly[:, columns[p]] - dot(mk[:, first * rows : last * rows], terms)

    ring = list(range(1, half)) + [0]
    for t in reversed(range(mid)):
        first_block = block_start(t, levels)
        second, kept = {}, {}
        for p in reversed(own(t)):
            n = p - (blocks - counts[t])
            for s in range(t + 1, levels):
                need(s, p)

            def part_of(dest, p=p, n=n):
                cut = pl.ds(pl.multiple_of(dest * rows, LANES), rows)
                value = acc[t][dest, :, n * LANES : (n + 1) * LANES]
                for s in range(t + 1, levels):
                    value = value - dot(atr[first_block + s - t, cut], wide[s, p])
                return value

            first = {}
            for i in ring:
                dest = lax.rem(yy + i, half) * 2 + 1 - core
                ps[t][n, i] = part_of(dest).astype(BF)
                first[i] = copies.start(ps[t].at[n, i], pr[t].at[n, i], mate)
            for s in range(t + 1, levels):
                widen(s, p, t)
            for i in ring[:-1]:
                dest = lax.rem(yy + i, half) * 2 + core
                value = part_of(dest)
                first[i].wait_recv()
                qs[t][n, i - 1] = (value + pr[t][n, i].astype(F32)).astype(BF)
                second[p, i] = copies.start(
                    qs[t].at[n, i - 1], qr[t].at[n, i - 1], {"row": dest}
                )
            value = part_of(row)
            first[0].wait_recv()
            kept[p] = value + pr[t][n, 0].astype(F32)
            if t == 0 and levels > 1 and p != own(t)[0]:
                ly[:, columns[p]] = leaf_back(1, levels, p)
        for p in reversed(own(t)):
            n = p - (blocks - counts[t])
            value = kept[p]
            for i in ring[:-1]:
                second[p, i].wait_recv()
                value = value + qr[t][n, i - 1].astype(F32)
            wide[t, p] = value.astype(BF)
            widen(t, p, t)
            if t == 0 and levels > 1 and p == own(t)[-1]:
                ly[:, columns[own(t)[0]]] = leaf_back(1, levels, own(t)[0])
    for p in reversed(own(0)):
        leaf_out[:, columns[p]] = leaf_back(0, 1, p).astype(BF)
    for p in reversed(range(blocks - counts[0])):
        for s in range(1, levels):
            need(s, p)
        if levels > 1:
            ly[:, columns[p]] = leaf_back(1, levels, p)
    for s in range(levels):
        for p in own(0):
            out[s, :, columns[p]] = wide[s, p]
    for p in reversed(range(blocks - counts[0])):
        need(0, p)
        leaf_out[:, columns[p]] = leaf_back(0, 1, p).astype(BF)
        for s in range(levels):
            out[s, :, columns[p]] = wide[s, p]
    for copy in copies.all:
        copy.wait_send()


def solve(leaf_rhs, leaf_inv, coupling, pattern, anc_rhs, anc):
    levels, rows, cols = anc_rhs.shape
    leaf_rows = leaf_rhs.shape[0]
    supers, width = leaf_inv.shape[:2]
    n_row = lax.axis_size("row")
    half = n_row // 2
    blocks = cols // LANES
    counts, splits = plan(levels, cols)
    span = range(levels - 2)
    early = block_start(levels - 2, levels)
    strip, tall = LANES // n_row, n_row * rows
    less = max(half - 1, 1)
    scratch = [
        pltpu.VMEM(leaf_rhs.shape, BF),
        pltpu.VMEM(leaf_inv.shape, BF),
        pltpu.VMEM(coupling.shape, BF),
        pltpu.VMEM(anc_rhs.shape, F32),
        pltpu.VMEM((early,) + anc.shape[1:], BF),
        pltpu.VMEM((leaf_rows, cols), F32),
        pltpu.VMEM((leaf_rows, cols), BF),
        pltpu.VMEM((leaf_rows, levels * rows), BF),
        pltpu.VMEM((levels, rows, leaf_rows), BF),
        pltpu.VMEM((early, n_row * rows, rows), BF),
        pltpu.VMEM((levels, blocks, rows, LANES), F32),
        pltpu.VMEM((levels, blocks, rows, LANES), BF),
    ]
    scratch += [
        pltpu.VMEM((2, tall, tall), BF),
        pltpu.VMEM((2 * rows, tall), BF),
        pltpu.VMEM((2, 2, LANES, rows), BF),
        pltpu.VMEM((2, 2, strip, tall), BF),
        pltpu.VMEM((strip, tall), F32),
        pltpu.VMEM((strip, tall), BF),
        pltpu.VMEM((strip, tall), BF),
        pltpu.VMEM((2, strip, tall), BF),
        pltpu.VMEM((2, 2, LANES, rows), BF),
        pltpu.VMEM((half, strip, tall), BF),
        pltpu.VMEM((half * strip, 2 * rows), BF),
        pltpu.VMEM((half, strip, tall), F32),
        pltpu.VMEM((half, strip, tall), BF),
        pltpu.VMEM((half, strip, tall), BF),
    ]
    scratch += [pltpu.VMEM((counts[t], levels - t, rows, LANES), BF) for t in span]
    scratch += [pltpu.VMEM((counts[t], levels - t, rows, LANES), BF) for t in span]
    scratch += [pltpu.VMEM((counts[t], n_row, rows, LANES), BF) for t in span]
    scratch += [pltpu.VMEM((n_row, rows, counts[t] * LANES), F32) for t in span]
    scratch += [pltpu.VMEM((counts[t], half, rows, LANES), BF) for t in span]
    scratch += [pltpu.VMEM((counts[t], half, rows, LANES), BF) for t in span]
    scratch += [pltpu.VMEM((counts[t], less, rows, LANES), BF) for t in span]
    scratch += [pltpu.VMEM((counts[t], less, rows, LANES), BF) for t in span]
    total = copies_needed(levels, n_row, counts)
    scratch += [pltpu.SemaphoreType.DMA((total,)), pltpu.SemaphoreType.DMA((total,))]
    scratch += [pltpu.SemaphoreType.DMA((2 * levels + 6,))]
    away = pl.BlockSpec(memory_space=pl.ANY)
    return pl.pallas_call(
        functools.partial(kernel, (levels, n_row, blocks, supers, width)),
        out_shape=(
            jax.ShapeDtypeStruct((leaf_rows, cols), BF),
            jax.ShapeDtypeStruct((levels, rows, cols), BF),
        ),
        in_specs=[away, away, away, pl.BlockSpec(memory_space=pltpu.SMEM), away, away],
        out_specs=(pl.BlockSpec(memory_space=pltpu.VMEM),) * 2,
        scratch_shapes=scratch,
        compiler_params=pltpu.CompilerParams(collective_id=0, has_side_effects=True, vmem_limit_bytes=VMEM_BYTES),
        name="solve",
    )(leaf_rhs, leaf_inv, coupling, pattern, anc_rhs, anc)


def tail_kernel(inv, vb, solved, x_leaf, x_anc):
    count, width = inv.shape[:2]
    for k in range(count):
        part = slice(k * width, (k + 1) * width)
        x_leaf[part] = tdot(inv[k], vb[part])
    x_anc[...] = solved[...].astype(F32)


def tail(leaf_inv, leaf_vb, solved):
    supers, width = leaf_inv.shape[:2]
    leaf_rows, cols = leaf_vb.shape
    anc_rows = solved.shape[0]
    steps = 2 if supers % 2 == 0 and anc_rows % 32 == 0 else 1
    rows = [leaf_rows // steps, anc_rows // steps]
    flat = [pl.BlockSpec((n, cols), lambda i: (i, 0)) for n in rows]
    return pl.pallas_call(
        tail_kernel,
        grid=(steps,),
        out_shape=(
            jax.ShapeDtypeStruct((leaf_rows, cols), F32),
            jax.ShapeDtypeStruct((anc_rows, cols), F32),
        ),
        in_specs=[pl.BlockSpec((supers // steps, width, width), lambda i: (i, 0, 0))] + flat,
        out_specs=tuple(flat),
        name="tail",
    )(leaf_inv, leaf_vb, solved)


def body(leaf_rhs, leaf_inv, coupling, pattern, anc_rhs, anc_blocks):
    _, levels, rows, cols = anc_rhs.shape
    leaf_vb, solved = solve(
        leaf_rhs, leaf_inv, coupling.transpose(1, 0, 2), pattern.T, anc_rhs[0], anc_blocks[0]
    )
    x_leaf, x_anc = tail(leaf_inv, leaf_vb, solved.reshape(levels * rows, cols))
    return (x_leaf, x_anc.reshape(1, levels, rows, cols))


def solution(mesh):
    placed = (
        P(("layer", "row"), None),
        P(("layer", "row"), None, None),
        P(("layer", "row"), None, None),
        P(("layer", "row"), None),
        P("layer", None, "row", None),
        P("layer", None, "row", None),
    )
    return jax.shard_map(
        body,
        mesh=mesh,
        in_specs=placed,
        out_specs=(P(("layer", "row"), None), P("layer", None, "row", None)),
        check_vma=False,
    )
```

```python
import functools

import jax
import jax.numpy as jnp
from jax import lax
from jax.experimental import pallas as pl
from jax.experimental.pallas import tpu as pltpu
from jax.sharding import PartitionSpec as P

MESH = pl.DeviceIdType.MESH
LANES = 128
VMEM_BYTES = 56 * 2**20
PARTS = 8
BF, F32 = jnp.bfloat16, jnp.float32


def block_start(tree_level, level_total):
    return tree_level * level_total - tree_level * (tree_level - 1) // 2


def plan(levels, cols):
    counts, splits, count = [], [], cols // LANES
    for _ in range(levels):
        split = count % 2 == 0
        count = count // 2 if split else count
        counts.append(count)
        splits.append(split)
    return counts, splits


def tdot(a, b):
    return lax.dot_general(a, b, (((0,), (0,)), ((), ())), preferred_element_type=F32)


def dot(a, b):
    return jnp.dot(a, b, preferred_element_type=F32)


def dot_t(a, b):
    return lax.dot_general(a, b, (((1,), (1,)), ((), ())), preferred_element_type=F32)


class Copies:
    def __init__(self, send, recv):
        self.send, self.recv, self.count, self.all = send, recv, 0, []

    def start(self, src, dst, device):
        copy = pltpu.make_async_remote_copy(
            src_ref=src,
            dst_ref=dst,
            send_sem=self.send.at[self.count],
            recv_sem=self.recv.at[self.count],
            device_id=device,
            device_id_type=MESH,
        )
        copy.start()
        self.count += 1
        self.all.append(copy)
        return copy


def copies_needed(levels, n_row, counts):
    half = n_row // 2
    total = 2 * (1 + 8 * (half - 1)) + 8 * n_row + 2 * half
    for t in range(levels - 2):
        total += counts[t] * (2 * (levels - t) + 1 + 2 * (half - 1) + half + half - 1)
    return total


def kernel(dims, rhs_in, inv_in, coup_in, pat, ancr_in, anc_in, leaf_out, out, inv_t, *scratch):
    levels, n_row, blocks, supers, width = dims
    rhs, inv, coup, ancr, anc, ly, yb, mk, mt, atr, pend, wide = scratch[:12]
    full, pair, xt, zr, kt, tt, rt, st, wr, zx, yx, pf, px, qx = scratch[12:26]
    used = 26
    mid, top = levels - 2, levels - 1
    groups = []
    for _ in range(8):
        groups.append(scratch[used : used + mid])
        used += mid
    tx, rx, zs, acc, ps, pr, qs, qr = groups
    send, recv, local = scratch[used:]
    counts, splits = plan(levels, blocks * LANES)
    rows = anc.shape[1]
    half = n_row // 2
    strip = LANES // n_row
    early = block_start(mid, levels)
    lay = lax.axis_index("layer")
    row = lax.axis_index("row")
    core = lax.rem(row, 2)
    yy = row // 2
    mate = {"row": yy * 2 + (1 - core)}
    bits = [lax.rem(lay // 2**t, 2) for t in range(levels)]
    across = [{"layer": lay + (1 - 2 * bits[t]) * 2**t} for t in range(levels)]

    def slab(r, part=0, parts=1):
        size = rows // parts
        return pl.ds(pl.multiple_of(r * rows + part * size, size), size)

    loads = {}

    def load(name, src, dst):
        loads[name] = pltpu.make_async_copy(src, dst, local.at[len(loads)])
        loads[name].start()

    load("rhs", rhs_in, rhs)
    load("inv", inv_in, inv)
    load("cross", anc_in.at[early + 1], full.at[0, slab(row)])
    for s in range(levels):
        load(("coup", s), coup_in.at[s], coup.at[s])
        load(("ancr", s), ancr_in.at[s], ancr.at[s])
    load("top", anc_in.at[early + 2], full.at[1, slab(row)])
    load("anc", anc_in.at[pl.ds(0, early)], anc)
    load("mid", anc_in.at[early], pair.at[slab(core)])

    barrier = pltpu.get_barrier_semaphore()
    peers = [{"row": lax.rem(row + i, n_row)} for i in range(n_row)]
    friends = [{**across[mid], **peer} for peer in peers]
    greet = peers[1:] + friends[1:] + across
    for other in greet:
        pl.semaphore_signal(barrier, inc=1, device_id=other, device_id_type=MESH)
    copies = Copies(send, recv)

    spread = {}
    way = [mid, 0]

    def sender(i):
        return lax.rem(yy - i + half, half) * 2 + core

    def push(key, k, where, device):
        spot = full.at[k, where]
        spread[key] = copies.start(spot, spot, device)

    def piece_of(r, k, q, mine):
        h = bits[way[k]] if mine else 1 - bits[way[k]]
        return slab(r, 2 * h + q, 4)

    def spread_first(k, q):
        def push_own(key, where_from, where_to, device):
            spread[key] = copies.start(
                anc_in.at[early + 1 + k, where_from], full.at[k, where_to], device
            )

        h = bits[way[k]]
        size = rows // 4
        src = pl.ds(pl.multiple_of((2 * h + q) * size, size), size)
        for i in range(1, half):
            other = {"row": lax.rem(yy + i, half) * 2 + core}
            push_own((k, q, "y", i), src, piece_of(row, k, q, True), other)
        if q == 0:
            push_own((k, "own"), pl.ds(0, rows), slab(row), mate)

    def spread_next(k, q):
        for i in range(1, half):
            spread[k, q, "y", i].wait_recv()
            where = piece_of(sender(i), k, q, True)
            push((k, q, "far", i), k, where, across[way[k]])
            push((k, q, "mate", i), k, where, mate)

    def spread_last(k, q):
        for i in range(1, half):
            spread[k, q, "far", i].wait_recv()
            push((k, q, "mate2", i), k, piece_of(sender(i), k, q, False), mate)

    def spread_done(k):
        spread[k, "own"].wait_recv()
        for q in range(2):
            for i in range(1, half):
                spread[k, q, "mate", i].wait_recv()
                spread[k, q, "mate2", i].wait_recv()

    order = list(range(counts[-1]))
    for t in reversed(range(levels)):
        if splits[t]:
            near = [bits[t] * counts[t] + j for j in order]
            order = [(1 - bits[t]) * counts[t] + j for j in order] + near
    columns = [pl.ds(pl.multiple_of(j * LANES, LANES), LANES) for j in order]

    def own(t):
        return list(range(blocks - counts[t], blocks))

    def theirs(t, p):
        return p - counts[t] if splits[t] else p

    pl.semaphore_wait(barrier, len(greet))
    spread_first(0, 0)
    spread_first(0, 1)
    halves = copies.start(anc_in.at[early], pair.at[slab(core)], mate)
    loads["rhs"].wait()
    loads["inv"].wait()
    for k in range(supers):
        part = slice(k * width, (k + 1) * width)
        value = dot(inv[k], rhs[part])
        ly[part] = value
        yb[part] = value.astype(BF)

    def mask(s):
        loads["coup", s].wait()
        cut = slice(s * rows, (s + 1) * rows)
        for k in range(supers):
            part = slice(k * width, (k + 1) * width)
            value = coup[s, part].astype(F32) * pat[s, k].astype(F32)
            mk[part, cut] = value.astype(BF)
            mt[s, :, part] = value.T.astype(BF)

    def share(s, where):
        if ("ancr", s) in loads:
            loads.pop(("ancr", s)).wait()
        for first in range(0, len(where), 2):
            two = where[first : first + 2]
            value = dot(mt[s], jnp.concatenate([yb[:, columns[p]] for p in two], axis=1))
            for n, p in enumerate(two):
                yield ancr[s, :, columns[p]] - value[:, n * LANES : (n + 1) * LANES]

    flight = {}

    def offer_urgent(t, p, value):
        n = p - (blocks - counts[t])
        tx[t][n, 0] = value.astype(BF)
        one = pl.ds(0, 1)
        flight[t, p, 0] = copies.start(tx[t].at[n, one], rx[t].at[n, one], across[t])

    def offer_rest(t, p, values):
        n = p - (blocks - counts[t])
        for k, value in enumerate(values):
            tx[t][n, 1 + k] = value.astype(BF)
            one = pl.ds(1 + k, 1)
            flight[t, p, 1 + k] = copies.start(tx[t].at[n, one], rx[t].at[n, one], across[t])

    mask(0)
    mine = own(0)
    away = [theirs(0, p) for p in mine]
    first_shares = list(share(0, away))
    for p, value in zip(mine, first_shares):
        offer_urgent(0, p, value)
    for p, value in zip(mine, share(0, mine)):
        pend[0, p] = value
    for s in range(1, levels):
        mask(s)
    later_shares = [list(share(s, away)) for s in range(1, levels)]
    for n, p in enumerate(mine):
        offer_rest(0, p, [values[n] for values in later_shares])
    for s in range(1, levels):
        for p, value in zip(mine, share(s, mine)):
            pend[s, p] = value
    loads["anc"].wait()
    spread_next(0, 0)

    def turn(k):
        for other in range(n_row):
            cut = slice(other * rows, (other + 1) * rows)
            atr[k, cut] = anc[k, :, cut].T

    kept_block = own(mid)[0]
    given_block = theirs(mid, kept_block)
    near, far = {}, {}

    def hand_over(j, p):
        b = 0 if p == kept_block else 1
        xt[b, j] = pend[mid + j, p].T.astype(BF)

        def piece(i):
            return xt.at[b, j, pl.ds(pl.multiple_of(peers[i]["row"] * strip, strip), strip)]

        if p == given_block:
            for i in range(n_row):
                far[j, i] = copies.start(piece(i), zr.at[1, j, :, slab(row)], friends[i])
        if p == kept_block:
            for i in range(1, n_row):
                near[j, i] = copies.start(piece(i), zr.at[0, j, :, slab(row)], peers[i])
            zr[0, j, :, slab(row)] = piece(0)[...]

    later_work = None
    for t in range(mid):
        first_block = block_start(t, levels)
        above = levels - t - 1
        if later_work is not None:
            later_work()
        gathers, to_mate = {}, {}
        for p in own(t):
            n = p - (blocks - counts[t])
            flight[t, p, 0].wait_recv()
            zs[t][n, row] = (pend[t, p] + rx[t][n, 0].astype(F32)).astype(BF)
            spot = zs[t].at[n, row]
            for i in range(1, half):
                other = lax.rem(yy + i, half) * 2 + core
                gathers[p, i] = copies.start(spot, spot, {"row": other})
            to_mate[p] = copies.start(spot, spot, mate)
        for s in range(t + 1, levels):
            turn(first_block + s - t)
        if t == 0:
            spread_next(0, 1)
            spread_first(1, 0)
        for p in own(t):
            n = p - (blocks - counts[t])

            def sums_of(slot, n=n):
                cut = pl.ds(pl.multiple_of(slot * rows, LANES), rows)
                return [
                    dot(anc[first_block + k, :, cut], zs[t][n, slot]) for k in range(1, above + 1)
                ]

            def add(old, new):
                return [a + b for a, b in zip(old, new)]

            total = sums_of(row)
            to_mate[p].wait_recv()
            total = add(total, sums_of(yy * 2 + 1 - core))
            passed = {}
            for i in range(1, half):
                gathers[p, i].wait_recv()
                origin = lax.rem(yy - i + half, half) * 2
                spot = zs[t].at[n, origin + core]
                passed[i] = copies.start(spot, spot, mate)
                total = add(total, sums_of(origin + core))
            for i in range(1, half):
                passed[i].wait_recv()
                origin = lax.rem(yy - i + half, half) * 2
                total = add(total, sums_of(origin + 1 - core))
            for k in range(above):
                flight[t, p, 1 + k].wait_recv()
                pend[t + 1 + k, p] = pend[t + 1 + k, p] + rx[t][n, 1 + k].astype(F32) - total[k]
                if t + 1 == mid:
                    hand_over(k, p)
            if t + 1 < mid:
                for q in own(t + 1):
                    if theirs(t + 1, q) == p:
                        offer_urgent(t + 1, q, pend[t + 1, p])
                        offer_rest(t + 1, q, [pend[s, p] for s in range(t + 2, levels)])

        def later_work(t=t, first_block=first_block):
            z_all = jnp.concatenate(
                [zs[t][n].reshape(n_row * rows, LANES) for n in range(counts[t])], axis=1
            )
            y_here = dot(anc[first_block], z_all).astype(BF)
            for other in range(n_row):
                acc[t][other] = tdot(anc[first_block, :, other * rows : (other + 1) * rows], y_here)

    spread_first(1, 1)
    later_work()
    for k in range(supers):
        inv_t[k] = inv[k].T
    spread_last(0, 0)
    spread_last(0, 1)
    for name in ("cross", "top", "mid"):
        loads[name].wait()
    halves.wait_recv()
    spread_next(1, 0)

    def gathered(j):
        for i in range(1, n_row):
            near[j, i].wait_recv()
        for i in range(n_row):
            far[j, i].wait_recv()
        return zr[0, j].astype(F32) + zr[1, j].astype(F32)

    z_mid = gathered(0).astype(BF)
    zx[yy] = z_mid
    asked = [
        copies.start(zx.at[yy], zx.at[yy], {"row": lax.rem(yy + i, half) * 2 + core})
        for i in range(1, half)
    ]
    spread_done(0)
    kt[...] = gathered(1) - dot_t(z_mid, full[0])
    tt[...] = kt[...].astype(BF)
    last = copies.start(tt, rt, across[top])
    spread_next(1, 1)
    spread_last(1, 0)
    for copy in asked:
        copy.wait_recv()
    tall = n_row * rows
    yx[...] = dot_t(zx[...].reshape(half * strip, tall), pair[...]).astype(BF)
    pf[...] = dot(yx[...], pair[...]).reshape(half, strip, tall)
    px[...] = pf[...].astype(BF)
    told = []
    for i in range(1, half):
        other = lax.rem(yy + i, half)
        told.append(copies.start(px.at[other], qx.at[yy], {"row": other * 2 + core}))
    spread_last(1, 1)
    spread_done(1)
    last.wait_recv()
    z_top = (kt[...] + rt[...].astype(F32)).astype(BF)
    y_top = dot_t(z_top, full[1]).astype(BF)
    back = {}

    def give_back(j):
        here = pl.ds(pl.multiple_of(row * strip, strip), strip)
        sides = [peers, friends] if splits[mid] else [peers]
        for side, group in enumerate(sides):
            for i in range(1 - side, n_row):
                part = st.at[j, :, slab(peers[i]["row"])]
                back[j, side, i] = copies.start(part, wr.at[j, side, here], group[i])
        wr[j, 0, here] = st[j, :, slab(row)]

    def take_back(j):
        for side, p in ((0, kept_block), (1, given_block)):
            if side == 0 or splits[mid]:
                for i in range(1 - side, n_row):
                    back[j, side, i].wait_recv()
                wide[mid + j, p] = wr[j, side].T

    st[1] = dot(y_top, full[1]).astype(BF)
    give_back(1)
    value = pf[yy] - dot(st[1], full[0])
    for copy in told:
        copy.wait_recv()
    for i in range(1, half):
        value = value + qx[lax.rem(yy + i, half)].astype(F32)
    st[0] = value.astype(BF)
    give_back(0)
    arriving = {}

    def need(s, p):
        copy = arriving.pop((s, p), None)
        if copy is not None:
            copy.wait_recv()

    def widen(s, p, t):
        if splits[t]:
            arriving[s, p - counts[t]] = copies.start(
                wide.at[s, p], wide.at[s, p - counts[t]], across[t]
            )

    def leaf_back(first, last, p):
        terms = jnp.concatenate([wide[s, p] for s in range(first, last)], axis=0)
        return ly[:, columns[p]] - dot(mk[:, first * rows : last * rows], terms)

    for j in (1, 0):
        take_back(j)
        for p in own(mid - 1):
            widen(mid + j, p, mid - 1)

    ring = list(range(1, half)) + [0]
    for t in reversed(range(mid)):
        first_block = block_start(t, levels)
        second, kept = {}, {}
        for p in reversed(own(t)):
            n = p - (blocks - counts[t])
            for s in range(t + 1, levels):
                need(s, p)

            def part_of(dest, p=p, n=n):
                cut = pl.ds(pl.multiple_of(dest * rows, LANES), rows)
                value = acc[t][dest, :, n * LANES : (n + 1) * LANES]
                for s in range(t + 1, levels):
                    value = value - dot(atr[first_block + s - t, cut], wide[s, p])
                return value

            first = {}
            for i in ring:
                dest = lax.rem(yy + i, half) * 2 + 1 - core
                ps[t][n, i] = part_of(dest).astype(BF)
                first[i] = copies.start(ps[t].at[n, i], pr[t].at[n, i], mate)
            for s in range(t + 1, levels if t + 1 < mid else mid):
                widen(s, p, t)
            for i in ring[:-1]:
                dest = lax.rem(yy + i, half) * 2 + core
                value = part_of(dest)
                first[i].wait_recv()
                qs[t][n, i - 1] = (value + pr[t][n, i].astype(F32)).astype(BF)
                second[p, i] = copies.start(
                    qs[t].at[n, i - 1], qr[t].at[n, i - 1], {"row": dest}
                )
            value = part_of(row)
            first[0].wait_recv()
            kept[p] = value + pr[t][n, 0].astype(F32)
            if t == 0 and levels > 1 and p != own(t)[0]:
                ly[:, columns[p]] = leaf_back(1, levels, p)
        for p in reversed(own(t)):
            n = p - (blocks - counts[t])
            value = kept[p]
            for i in ring[:-1]:
                second[p, i].wait_recv()
                value = value + qr[t][n, i - 1].astype(F32)
            wide[t, p] = value.astype(BF)
            widen(t, p, t)
            if t == 0 and levels > 1 and p == own(t)[-1]:
                ly[:, columns[own(t)[0]]] = leaf_back(1, levels, own(t)[0])
    for p in reversed(own(0)):
        leaf_out[:, columns[p]] = leaf_back(0, 1, p).astype(BF)
    for p in reversed(range(blocks - counts[0])):
        for s in range(1, levels):
            need(s, p)
        if levels > 1:
            ly[:, columns[p]] = leaf_back(1, levels, p)
    for s in range(levels):
        for p in own(0):
            out[s * rows : (s + 1) * rows, columns[p]] = wide[s, p]
    for p in reversed(range(blocks - counts[0])):
        need(0, p)
        leaf_out[:, columns[p]] = leaf_back(0, 1, p).astype(BF)
        for s in range(levels):
            out[s * rows : (s + 1) * rows, columns[p]] = wide[s, p]
    for copy in copies.all:
        copy.wait_send()


def solve(leaf_rhs, leaf_inv, coupling, pattern, anc_rhs, anc):
    levels, rows, cols = anc_rhs.shape
    leaf_rows = leaf_rhs.shape[0]
    supers, width = leaf_inv.shape[:2]
    n_row = lax.axis_size("row")
    half = n_row // 2
    blocks = cols // LANES
    counts, splits = plan(levels, cols)
    span = range(levels - 2)
    early = block_start(levels - 2, levels)
    strip, tall = LANES // n_row, n_row * rows
    less = max(half - 1, 1)
    scratch = [
        pltpu.VMEM(leaf_rhs.shape, BF),
        pltpu.VMEM(leaf_inv.shape, BF),
        pltpu.VMEM(coupling.shape, BF),
        pltpu.VMEM(anc_rhs.shape, F32),
        pltpu.VMEM((early,) + anc.shape[1:], BF),
        pltpu.VMEM((leaf_rows, cols), F32),
        pltpu.VMEM((leaf_rows, cols), BF),
        pltpu.VMEM((leaf_rows, levels * rows), BF),
        pltpu.VMEM((levels, rows, leaf_rows), BF),
        pltpu.VMEM((early, n_row * rows, rows), BF),
        pltpu.VMEM((levels, blocks, rows, LANES), F32),
        pltpu.VMEM((levels, blocks, rows, LANES), BF),
    ]
    scratch += [
        pltpu.VMEM((2, tall, tall), BF),
        pltpu.VMEM((2 * rows, tall), BF),
        pltpu.VMEM((2, 2, LANES, rows), BF),
        pltpu.VMEM((2, 2, strip, tall), BF),
        pltpu.VMEM((strip, tall), F32),
        pltpu.VMEM((strip, tall), BF),
        pltpu.VMEM((strip, tall), BF),
        pltpu.VMEM((2, strip, tall), BF),
        pltpu.VMEM((2, 2, LANES, rows), BF),
        pltpu.VMEM((half, strip, tall), BF),
        pltpu.VMEM((half * strip, 2 * rows), BF),
        pltpu.VMEM((half, strip, tall), F32),
        pltpu.VMEM((half, strip, tall), BF),
        pltpu.VMEM((half, strip, tall), BF),
    ]
    scratch += [pltpu.VMEM((counts[t], levels - t, rows, LANES), BF) for t in span]
    scratch += [pltpu.VMEM((counts[t], levels - t, rows, LANES), BF) for t in span]
    scratch += [pltpu.VMEM((counts[t], n_row, rows, LANES), BF) for t in span]
    scratch += [pltpu.VMEM((n_row, rows, counts[t] * LANES), F32) for t in span]
    scratch += [pltpu.VMEM((counts[t], half, rows, LANES), BF) for t in span]
    scratch += [pltpu.VMEM((counts[t], half, rows, LANES), BF) for t in span]
    scratch += [pltpu.VMEM((counts[t], less, rows, LANES), BF) for t in span]
    scratch += [pltpu.VMEM((counts[t], less, rows, LANES), BF) for t in span]
    total = copies_needed(levels, n_row, counts)
    scratch += [pltpu.SemaphoreType.DMA((total,)), pltpu.SemaphoreType.DMA((total,))]
    scratch += [pltpu.SemaphoreType.DMA((2 * levels + 6,))]
    away = pl.BlockSpec(memory_space=pl.ANY)
    return pl.pallas_call(
        functools.partial(kernel, (levels, n_row, blocks, supers, width)),
        out_shape=(
            pltpu.VMEM((leaf_rows, cols), BF),
            pltpu.VMEM((levels * rows, cols), BF),
            pltpu.VMEM(leaf_inv.shape, BF),
        ),
        in_specs=[away, away, away, pl.BlockSpec(memory_space=pltpu.SMEM), away, away],
        out_specs=(pl.BlockSpec(memory_space=pltpu.VMEM),) * 3,
        scratch_shapes=scratch,
        compiler_params=pltpu.CompilerParams(collective_id=0, has_side_effects=True, vmem_limit_bytes=VMEM_BYTES),
        name="solve",
    )(leaf_rhs, leaf_inv, coupling, pattern, anc_rhs, anc)


def tail_kernel(inv_t, vb, solved, x_leaf, x_anc, leaf, anc, sems):
    count, width = inv_t.shape[:2]
    size = anc.shape[0] // PARTS
    copies = []

    def finish(src, dst, part):
        copy = pltpu.make_async_copy(src.at[part], dst.at[part], sems.at[len(copies)])
        copy.start()
        copies.append(copy)

    for k in range(PARTS):
        part = pl.ds(k * size, size)
        anc[part] = solved[part].astype(F32)
        finish(anc, x_anc, part)
    for k in range(count):
        part = pl.ds(k * width, width)
        leaf[part] = dot(inv_t[k], vb[part])
        finish(leaf, x_leaf, part)
    for copy in copies:
        copy.wait()


def tail(inv_t, leaf_vb, solved):
    count = inv_t.shape[0]
    result = (
        jax.ShapeDtypeStruct(leaf_vb.shape, F32),
        jax.ShapeDtypeStruct(solved.shape, F32),
    )
    return pl.pallas_call(
        tail_kernel,
        out_shape=result,
        in_specs=[pl.BlockSpec(memory_space=pltpu.VMEM)] * 3,
        out_specs=(pl.BlockSpec(memory_space=pl.ANY),) * 2,
        scratch_shapes=[
            pltpu.VMEM(leaf_vb.shape, F32),
            pltpu.VMEM(solved.shape, F32),
            pltpu.SemaphoreType.DMA((count + PARTS,)),
        ],
        name="tail",
    )(inv_t, leaf_vb, solved)


def body(leaf_rhs, leaf_inv, coupling, pattern, anc_rhs, anc_blocks):
    _, levels, rows, cols = anc_rhs.shape
    leaf_vb, solved, inv_t = solve(
        leaf_rhs, leaf_inv, coupling.transpose(1, 0, 2), pattern.T, anc_rhs[0], anc_blocks[0]
    )
    leaf_vb = pltpu.with_memory_space_constraint(leaf_vb, pltpu.VMEM)
    solved = pltpu.with_memory_space_constraint(solved, pltpu.VMEM)
    inv_t = pltpu.with_memory_space_constraint(inv_t, pltpu.VMEM)
    x_leaf, x_anc = tail(inv_t, leaf_vb, solved)
    return (x_leaf, x_anc.reshape(1, levels, rows, cols))


def solution(mesh):
    placed = (
        P(("layer", "row"), None),
        P(("layer", "row"), None, None),
        P(("layer", "row"), None, None),
        P(("layer", "row"), None),
        P("layer", None, "row", None),
        P("layer", None, "row", None),
    )
    return jax.shard_map(
        body,
        mesh=mesh,
        in_specs=placed,
        out_specs=(P(("layer", "row"), None), P("layer", None, "row", None)),
        check_vma=False,
    )
```

```python
import functools

import jax
import jax.numpy as jnp
from jax import lax
from jax.experimental import pallas as pl
from jax.experimental.pallas import tpu as pltpu
from jax.sharding import PartitionSpec as P

MESH = pl.DeviceIdType.MESH
LANES = 128
PIECES = 4
VMEM_BYTES = 56 * 2**20
PARTS = 8
BF, F32 = jnp.bfloat16, jnp.float32


def block_start(tree_level, level_total):
    return tree_level * level_total - tree_level * (tree_level - 1) // 2


def plan(levels, cols):
    counts, splits, count = [], [], cols // LANES
    for _ in range(levels):
        split = count % 2 == 0
        count = count // 2 if split else count
        counts.append(count)
        splits.append(split)
    return counts, splits


def tdot(a, b):
    return lax.dot_general(a, b, (((0,), (0,)), ((), ())), preferred_element_type=F32)


def dot(a, b):
    return jnp.dot(a, b, preferred_element_type=F32)


def dot_t(a, b):
    return lax.dot_general(a, b, (((1,), (1,)), ((), ())), preferred_element_type=F32)


class Copies:
    def __init__(self, send, recv):
        self.send, self.recv, self.count, self.all = send, recv, 0, []

    def start(self, src, dst, device):
        copy = pltpu.make_async_remote_copy(
            src_ref=src,
            dst_ref=dst,
            send_sem=self.send.at[self.count],
            recv_sem=self.recv.at[self.count],
            device_id=device,
            device_id_type=MESH,
        )
        copy.start()
        self.count += 1
        self.all.append(copy)
        return copy


def copies_needed(levels, n_row, counts):
    half = n_row // 2
    total = 2 * (1 + 4 * PIECES * (half - 1)) + 8 * n_row + 2 * half
    for t in range(levels - 2):
        total += counts[t] * (2 * (levels - t) + 1 + 2 * (half - 1) + half + half - 1)
    return total


def kernel(dims, rhs_in, inv_in, coup_in, pat, ancr_in, anc_in, leaf_out, out, inv_t, *scratch):
    levels, n_row, blocks, supers, width = dims
    rhs, inv, coup, ancr, anc, ly, yb, mk, mt, atr, pend, wide = scratch[:12]
    full, pair, xt, zr, kt, tt, rt, st, wr, zx, yx, pf, px, qx, tt2, yt = scratch[12:28]
    used = 28
    mid, top = levels - 2, levels - 1
    groups = []
    for _ in range(8):
        groups.append(scratch[used : used + mid])
        used += mid
    tx, rx, zs, acc, ps, pr, qs, qr = groups
    send, recv, local = scratch[used:]
    counts, splits = plan(levels, blocks * LANES)
    rows = anc.shape[1]
    half = n_row // 2
    strip = LANES // n_row
    early = block_start(mid, levels)
    lay = lax.axis_index("layer")
    row = lax.axis_index("row")
    core = lax.rem(row, 2)
    yy = row // 2
    mate = {"row": yy * 2 + (1 - core)}
    bits = [lax.rem(lay // 2**t, 2) for t in range(levels)]
    across = [{"layer": lay + (1 - 2 * bits[t]) * 2**t} for t in range(levels)]

    def slab(r, part=0, parts=1):
        size = rows // parts
        return pl.ds(pl.multiple_of(r * rows + part * size, size), size)

    loads = {}

    def load(name, src, dst):
        loads[name] = pltpu.make_async_copy(src, dst, local.at[len(loads)])
        loads[name].start()

    load("rhs", rhs_in, rhs)
    load("inv", inv_in, inv)
    load("cross", anc_in.at[early + 1], full.at[0, slab(row)])
    for s in range(levels):
        load(("coup", s), coup_in.at[s], coup.at[s])
        load(("ancr", s), ancr_in.at[s], ancr.at[s])
    load("top", anc_in.at[early + 2], full.at[1, slab(row)])
    load("anc", anc_in.at[pl.ds(0, early)], anc)
    load("mid", anc_in.at[early], pair.at[slab(core)])

    barrier = pltpu.get_barrier_semaphore()
    peers = [{"row": lax.rem(row + i, n_row)} for i in range(n_row)]
    friends = [{**across[mid], **peer} for peer in peers]
    greet = peers[1:] + friends[1:] + across
    for other in greet:
        pl.semaphore_signal(barrier, inc=1, device_id=other, device_id_type=MESH)
    copies = Copies(send, recv)

    spread = {}
    way = [mid, 0]

    def sender(i):
        return lax.rem(yy - i + half, half) * 2 + core

    def push(key, k, where, device):
        spot = full.at[k, where]
        spread[key] = copies.start(spot, spot, device)

    def piece_of(r, k, q, mine):
        h = bits[way[k]] if mine else 1 - bits[way[k]]
        return slab(r, PIECES * h + q, 2 * PIECES)

    def spread_first(k, q):
        def push_own(key, where_from, where_to, device):
            spread[key] = copies.start(
                anc_in.at[early + 1 + k, where_from], full.at[k, where_to], device
            )

        h = bits[way[k]]
        size = rows // (2 * PIECES)
        src = pl.ds(pl.multiple_of((PIECES * h + q) * size, size), size)
        for i in range(1, half):
            other = {"row": lax.rem(yy + i, half) * 2 + core}
            push_own((k, q, "y", i), src, piece_of(row, k, q, True), other)
        if q == 0:
            push_own((k, "own"), pl.ds(0, rows), slab(row), mate)

    def spread_next(k, q):
        for i in range(1, half):
            spread[k, q, "y", i].wait_recv()
            where = piece_of(sender(i), k, q, True)
            push((k, q, "far", i), k, where, across[way[k]])
            push((k, q, "mate", i), k, where, mate)

    def spread_last(k, q):
        for i in range(1, half):
            spread[k, q, "far", i].wait_recv()
            push((k, q, "mate2", i), k, piece_of(sender(i), k, q, False), mate)

    def spread_done(k):
        spread[k, "own"].wait_recv()
        for q in range(PIECES):
            for i in range(1, half):
                spread[k, q, "mate", i].wait_recv()
                spread[k, q, "mate2", i].wait_recv()

    order = list(range(counts[-1]))
    for t in reversed(range(levels)):
        if splits[t]:
            near = [bits[t] * counts[t] + j for j in order]
            order = [(1 - bits[t]) * counts[t] + j for j in order] + near
    columns = [pl.ds(pl.multiple_of(j * LANES, LANES), LANES) for j in order]

    def own(t):
        return list(range(blocks - counts[t], blocks))

    def theirs(t, p):
        return p - counts[t] if splits[t] else p

    pl.semaphore_wait(barrier, len(greet))
    for q in range(PIECES // 2):
        spread_first(0, q)
    for q in range(PIECES // 2, PIECES):
        spread_first(0, q)
    halves = copies.start(anc_in.at[early], pair.at[slab(core)], mate)
    loads["rhs"].wait()
    loads["inv"].wait()
    for k in range(supers):
        part = slice(k * width, (k + 1) * width)
        value = dot(inv[k], rhs[part])
        ly[part] = value
        yb[part] = value.astype(BF)

    def mask(s):
        loads["coup", s].wait()
        cut = slice(s * rows, (s + 1) * rows)
        for k in range(supers):
            part = slice(k * width, (k + 1) * width)
            value = coup[s, part].astype(F32) * pat[s, k].astype(F32)
            mk[part, cut] = value.astype(BF)
            mt[s, :, part] = value.T.astype(BF)

    def share(s, where):
        if ("ancr", s) in loads:
            loads.pop(("ancr", s)).wait()
        for first in range(0, len(where), 2):
            two = where[first : first + 2]
            value = dot(mt[s], jnp.concatenate([yb[:, columns[p]] for p in two], axis=1))
            for n, p in enumerate(two):
                yield ancr[s, :, columns[p]] - value[:, n * LANES : (n + 1) * LANES]

    flight = {}

    def offer_urgent(t, p, value):
        n = p - (blocks - counts[t])
        tx[t][n, 0] = value.astype(BF)
        one = pl.ds(0, 1)
        flight[t, p, 0] = copies.start(tx[t].at[n, one], rx[t].at[n, one], across[t])

    def offer_rest(t, p, values):
        n = p - (blocks - counts[t])
        for k, value in enumerate(values):
            tx[t][n, 1 + k] = value.astype(BF)
            one = pl.ds(1 + k, 1)
            flight[t, p, 1 + k] = copies.start(tx[t].at[n, one], rx[t].at[n, one], across[t])

    mask(0)
    mine = own(0)
    away = [theirs(0, p) for p in mine]
    first_shares = list(share(0, away))
    for p, value in zip(mine, first_shares):
        offer_urgent(0, p, value)
    for p, value in zip(mine, share(0, mine)):
        pend[0, p] = value
    for s in range(1, levels):
        mask(s)
    later_shares = [list(share(s, away)) for s in range(1, levels)]
    for n, p in enumerate(mine):
        offer_rest(0, p, [values[n] for values in later_shares])
    for s in range(1, levels):
        for p, value in zip(mine, share(s, mine)):
            pend[s, p] = value
    loads["anc"].wait()
    for q in range(PIECES // 2):
        spread_next(0, q)

    def turn(k):
        for other in range(n_row):
            cut = slice(other * rows, (other + 1) * rows)
            atr[k, cut] = anc[k, :, cut].T

    kept_block = own(mid)[0]
    given_block = theirs(mid, kept_block)
    near, far = {}, {}

    def hand_over(j, p):
        b = 0 if p == kept_block else 1
        xt[b, j] = pend[mid + j, p].T.astype(BF)

        def piece(i):
            return xt.at[b, j, pl.ds(pl.multiple_of(peers[i]["row"] * strip, strip), strip)]

        if p == given_block:
            for i in range(n_row):
                far[j, i] = copies.start(piece(i), zr.at[1, j, :, slab(row)], friends[i])
        if p == kept_block:
            for i in range(1, n_row):
                near[j, i] = copies.start(piece(i), zr.at[0, j, :, slab(row)], peers[i])
            zr[0, j, :, slab(row)] = piece(0)[...]

    later_work = None
    for t in range(mid):
        first_block = block_start(t, levels)
        above = levels - t - 1
        if later_work is not None:
            later_work()
        gathers, to_mate = {}, {}
        for p in own(t):
            n = p - (blocks - counts[t])
            flight[t, p, 0].wait_recv()
            zs[t][n, row] = (pend[t, p] + rx[t][n, 0].astype(F32)).astype(BF)
            spot = zs[t].at[n, row]
            for i in range(1, half):
                other = lax.rem(yy + i, half) * 2 + core
                gathers[p, i] = copies.start(spot, spot, {"row": other})
            to_mate[p] = copies.start(spot, spot, mate)
        for s in range(t + 1, levels):
            turn(first_block + s - t)
        if t == 0:
            for q in range(PIECES // 2, PIECES):
                spread_next(0, q)
            for q in range(PIECES // 2):
                spread_first(1, q)
        for p in own(t):
            n = p - (blocks - counts[t])

            def sums_of(slot, n=n):
                cut = pl.ds(pl.multiple_of(slot * rows, LANES), rows)
                return [
                    dot(anc[first_block + k, :, cut], zs[t][n, slot]) for k in range(1, above + 1)
                ]

            def add(old, new):
                return [a + b for a, b in zip(old, new)]

            total = sums_of(row)
            to_mate[p].wait_recv()
            total = add(total, sums_of(yy * 2 + 1 - core))
            passed = {}
            for i in range(1, half):
                gathers[p, i].wait_recv()
                origin = lax.rem(yy - i + half, half) * 2
                spot = zs[t].at[n, origin + core]
                passed[i] = copies.start(spot, spot, mate)
                total = add(total, sums_of(origin + core))
            for i in range(1, half):
                passed[i].wait_recv()
                origin = lax.rem(yy - i + half, half) * 2
                total = add(total, sums_of(origin + 1 - core))
            for k in range(above):
                flight[t, p, 1 + k].wait_recv()
                pend[t + 1 + k, p] = pend[t + 1 + k, p] + rx[t][n, 1 + k].astype(F32) - total[k]
                if t + 1 == mid:
                    hand_over(k, p)
            if t + 1 < mid:
                for q in own(t + 1):
                    if theirs(t + 1, q) == p:
                        offer_urgent(t + 1, q, pend[t + 1, p])
                        offer_rest(t + 1, q, [pend[s, p] for s in range(t + 2, levels)])

        def later_work(t=t, first_block=first_block):
            z_all = jnp.concatenate(
                [zs[t][n].reshape(n_row * rows, LANES) for n in range(counts[t])], axis=1
            )
            y_here = dot(anc[first_block], z_all).astype(BF)
            for other in range(n_row):
                acc[t][other] = tdot(anc[first_block, :, other * rows : (other + 1) * rows], y_here)

    for q in range(PIECES // 2, PIECES):
        spread_first(1, q)
    later_work()
    for k in range(supers):
        inv_t[k] = inv[k].T
    for q in range(PIECES // 2):
        spread_last(0, q)
    for q in range(PIECES // 2, PIECES):
        spread_last(0, q)
    for name in ("cross", "top", "mid"):
        loads[name].wait()
    halves.wait_recv()
    for q in range(PIECES // 2):
        spread_next(1, q)

    def gathered(j):
        for i in range(1, n_row):
            near[j, i].wait_recv()
        for i in range(n_row):
            far[j, i].wait_recv()
        return zr[0, j].astype(F32) + zr[1, j].astype(F32)

    cuts = [slice(0, half * rows), slice(half * rows, n_row * rows)]
    z_mid = gathered(0).astype(BF)
    zx[yy] = z_mid
    asked = [
        copies.start(zx.at[yy], zx.at[yy], {"row": lax.rem(yy + i, half) * 2 + core})
        for i in range(1, half)
    ]
    spread_done(0)
    mixed = gathered(1)
    last = []
    for cut in cuts:
        kt[:, cut] = mixed[:, cut] - dot_t(z_mid, full[0, cut])
        tt[:, cut] = kt[:, cut].astype(BF)
        last.append(copies.start(tt.at[:, cut], rt.at[:, cut], across[top]))
    for q in range(PIECES // 2, PIECES):
        spread_next(1, q)
    for q in range(PIECES // 2):
        spread_last(1, q)
    for copy in asked:
        copy.wait_recv()
    tall = n_row * rows
    yx[...] = dot_t(zx[...].reshape(half * strip, tall), pair[...]).astype(BF)
    pf[...] = dot(yx[...], pair[...]).reshape(half, strip, tall)
    px[...] = pf[...].astype(BF)
    told = []
    for i in range(1, half):
        other = lax.rem(yy + i, half)
        told.append(copies.start(px.at[other], qx.at[yy], {"row": other * 2 + core}))
    for q in range(PIECES // 2, PIECES):
        spread_last(1, q)
    spread_done(1)
    for side, copy in enumerate(last):
        copy.wait_recv()
        cut = cuts[side]
        tt2[:, cut] = (kt[:, cut] + rt[:, cut].astype(F32)).astype(BF)
        for r in range(side * half, (side + 1) * half):
            part = slice(r * rows, (r + 1) * rows)
            reach = slice(0, (r + 1) * rows)
            yt[:, part] = dot_t(tt2[:, reach], full[1, part, reach]).astype(BF)
    back = {}

    def give_back(j):
        here = pl.ds(pl.multiple_of(row * strip, strip), strip)
        sides = [peers, friends] if splits[mid] else [peers]
        for side, group in enumerate(sides):
            for i in range(1 - side, n_row):
                part = st.at[j, :, slab(peers[i]["row"])]
                back[j, side, i] = copies.start(part, wr.at[j, side, here], group[i])
        wr[j, 0, here] = st[j, :, slab(row)]

    def take_back(j):
        for side, p in ((0, kept_block), (1, given_block)):
            if side == 0 or splits[mid]:
                for i in range(1 - side, n_row):
                    back[j, side, i].wait_recv()
                wide[mid + j, p] = wr[j, side].T

    for r in range(n_row):
        part = slice(r * rows, (r + 1) * rows)
        below = slice(r * rows, n_row * rows)
        st[1, :, part] = dot(yt[:, below], full[1, below, part]).astype(BF)
    give_back(1)
    value = pf[yy] - dot(st[1], full[0])
    for copy in told:
        copy.wait_recv()
    for i in range(1, half):
        value = value + qx[lax.rem(yy + i, half)].astype(F32)
    st[0] = value.astype(BF)
    give_back(0)
    arriving = {}

    def need(s, p):
        copy = arriving.pop((s, p), None)
        if copy is not None:
            copy.wait_recv()

    def widen(s, p, t):
        if splits[t]:
            arriving[s, p - counts[t]] = copies.start(
                wide.at[s, p], wide.at[s, p - counts[t]], across[t]
            )

    def leaf_back(first, last, p):
        terms = jnp.concatenate([wide[s, p] for s in range(first, last)], axis=0)
        return ly[:, columns[p]] - dot(mk[:, first * rows : last * rows], terms)

    for j in (1, 0):
        take_back(j)
        for p in own(mid - 1):
            widen(mid + j, p, mid - 1)

    ring = list(range(1, half)) + [0]
    for t in reversed(range(mid)):
        first_block = block_start(t, levels)
        second, kept = {}, {}
        for p in reversed(own(t)):
            n = p - (blocks - counts[t])
            for s in range(t + 1, levels):
                need(s, p)

            def part_of(dest, p=p, n=n):
                cut = pl.ds(pl.multiple_of(dest * rows, LANES), rows)
                value = acc[t][dest, :, n * LANES : (n + 1) * LANES]
                for s in range(t + 1, levels):
                    value = value - dot(atr[first_block + s - t, cut], wide[s, p])
                return value

            first = {}
            for i in ring:
                dest = lax.rem(yy + i, half) * 2 + 1 - core
                ps[t][n, i] = part_of(dest).astype(BF)
                first[i] = copies.start(ps[t].at[n, i], pr[t].at[n, i], mate)
            for s in range(t + 1, levels if t + 1 < mid else mid):
                widen(s, p, t)
            for i in ring[:-1]:
                dest = lax.rem(yy + i, half) * 2 + core
                value = part_of(dest)
                first[i].wait_recv()
                qs[t][n, i - 1] = (value + pr[t][n, i].astype(F32)).astype(BF)
                second[p, i] = copies.start(
                    qs[t].at[n, i - 1], qr[t].at[n, i - 1], {"row": dest}
                )
            value = part_of(row)
            first[0].wait_recv()
            kept[p] = value + pr[t][n, 0].astype(F32)
            if t == 0 and levels > 1 and p != own(t)[0]:
                ly[:, columns[p]] = leaf_back(1, levels, p)
        for p in reversed(own(t)):
            n = p - (blocks - counts[t])
            value = kept[p]
            for i in ring[:-1]:
                second[p, i].wait_recv()
                value = value + qr[t][n, i - 1].astype(F32)
            wide[t, p] = value.astype(BF)
            widen(t, p, t)
            if t == 0 and levels > 1 and p == own(t)[-1]:
                ly[:, columns[own(t)[0]]] = leaf_back(1, levels, own(t)[0])
    for p in reversed(own(0)):
        leaf_out[:, columns[p]] = leaf_back(0, 1, p).astype(BF)
    for p in reversed(range(blocks - counts[0])):
        for s in range(1, levels):
            need(s, p)
        if levels > 1:
            ly[:, columns[p]] = leaf_back(1, levels, p)
    for s in range(levels):
        for p in own(0):
            out[s * rows : (s + 1) * rows, columns[p]] = wide[s, p]
    for p in reversed(range(blocks - counts[0])):
        need(0, p)
        leaf_out[:, columns[p]] = leaf_back(0, 1, p).astype(BF)
        for s in range(levels):
            out[s * rows : (s + 1) * rows, columns[p]] = wide[s, p]
    for copy in copies.all:
        copy.wait_send()


def solve(leaf_rhs, leaf_inv, coupling, pattern, anc_rhs, anc):
    levels, rows, cols = anc_rhs.shape
    leaf_rows = leaf_rhs.shape[0]
    supers, width = leaf_inv.shape[:2]
    n_row = lax.axis_size("row")
    half = n_row // 2
    blocks = cols // LANES
    counts, splits = plan(levels, cols)
    span = range(levels - 2)
    early = block_start(levels - 2, levels)
    strip, tall = LANES // n_row, n_row * rows
    less = max(half - 1, 1)
    scratch = [
        pltpu.VMEM(leaf_rhs.shape, BF),
        pltpu.VMEM(leaf_inv.shape, BF),
        pltpu.VMEM(coupling.shape, BF),
        pltpu.VMEM(anc_rhs.shape, F32),
        pltpu.VMEM((early,) + anc.shape[1:], BF),
        pltpu.VMEM((leaf_rows, cols), F32),
        pltpu.VMEM((leaf_rows, cols), BF),
        pltpu.VMEM((leaf_rows, levels * rows), BF),
        pltpu.VMEM((levels, rows, leaf_rows), BF),
        pltpu.VMEM((early, n_row * rows, rows), BF),
        pltpu.VMEM((levels, blocks, rows, LANES), F32),
        pltpu.VMEM((levels, blocks, rows, LANES), BF),
    ]
    scratch += [
        pltpu.VMEM((2, tall, tall), BF),
        pltpu.VMEM((2 * rows, tall), BF),
        pltpu.VMEM((2, 2, LANES, rows), BF),
        pltpu.VMEM((2, 2, strip, tall), BF),
        pltpu.VMEM((strip, tall), F32),
        pltpu.VMEM((strip, tall), BF),
        pltpu.VMEM((strip, tall), BF),
        pltpu.VMEM((2, strip, tall), BF),
        pltpu.VMEM((2, 2, LANES, rows), BF),
        pltpu.VMEM((half, strip, tall), BF),
        pltpu.VMEM((half * strip, 2 * rows), BF),
        pltpu.VMEM((half, strip, tall), F32),
        pltpu.VMEM((half, strip, tall), BF),
        pltpu.VMEM((half, strip, tall), BF),
        pltpu.VMEM((strip, tall), BF),
        pltpu.VMEM((strip, tall), BF),
    ]
    scratch += [pltpu.VMEM((counts[t], levels - t, rows, LANES), BF) for t in span]
    scratch += [pltpu.VMEM((counts[t], levels - t, rows, LANES), BF) for t in span]
    scratch += [pltpu.VMEM((counts[t], n_row, rows, LANES), BF) for t in span]
    scratch += [pltpu.VMEM((n_row, rows, counts[t] * LANES), F32) for t in span]
    scratch += [pltpu.VMEM((counts[t], half, rows, LANES), BF) for t in span]
    scratch += [pltpu.VMEM((counts[t], half, rows, LANES), BF) for t in span]
    scratch += [pltpu.VMEM((counts[t], less, rows, LANES), BF) for t in span]
    scratch += [pltpu.VMEM((counts[t], less, rows, LANES), BF) for t in span]
    total = copies_needed(levels, n_row, counts)
    scratch += [pltpu.SemaphoreType.DMA((total,)), pltpu.SemaphoreType.DMA((total,))]
    scratch += [pltpu.SemaphoreType.DMA((2 * levels + 6,))]
    away = pl.BlockSpec(memory_space=pl.ANY)
    return pl.pallas_call(
        functools.partial(kernel, (levels, n_row, blocks, supers, width)),
        out_shape=(
            pltpu.VMEM((leaf_rows, cols), BF),
            pltpu.VMEM((levels * rows, cols), BF),
            pltpu.VMEM(leaf_inv.shape, BF),
        ),
        in_specs=[away, away, away, pl.BlockSpec(memory_space=pltpu.SMEM), away, away],
        out_specs=(pl.BlockSpec(memory_space=pltpu.VMEM),) * 3,
        scratch_shapes=scratch,
        compiler_params=pltpu.CompilerParams(collective_id=0, has_side_effects=True, vmem_limit_bytes=VMEM_BYTES),
        name="solve",
    )(leaf_rhs, leaf_inv, coupling, pattern, anc_rhs, anc)


def tail_kernel(inv_t, vb, solved, x_leaf, x_anc, leaf, anc, sems):
    count, width = inv_t.shape[:2]
    size = anc.shape[0] // PARTS
    copies = []

    def finish(src, dst, part):
        copy = pltpu.make_async_copy(src.at[part], dst.at[part], sems.at[len(copies)])
        copy.start()
        copies.append(copy)

    for k in range(PARTS):
        part = pl.ds(k * size, size)
        anc[part] = solved[part].astype(F32)
        finish(anc, x_anc, part)
    for k in range(count):
        part = pl.ds(k * width, width)
        leaf[part] = dot(inv_t[k], vb[part])
        finish(leaf, x_leaf, part)
    for copy in copies:
        copy.wait()


def tail(inv_t, leaf_vb, solved):
    count = inv_t.shape[0]
    result = (
        jax.ShapeDtypeStruct(leaf_vb.shape, F32),
        jax.ShapeDtypeStruct(solved.shape, F32),
    )
    return pl.pallas_call(
        tail_kernel,
        out_shape=result,
        in_specs=[pl.BlockSpec(memory_space=pltpu.VMEM)] * 3,
        out_specs=(pl.BlockSpec(memory_space=pl.ANY),) * 2,
        scratch_shapes=[
            pltpu.VMEM(leaf_vb.shape, F32),
            pltpu.VMEM(solved.shape, F32),
            pltpu.SemaphoreType.DMA((count + PARTS,)),
        ],
        name="tail",
    )(inv_t, leaf_vb, solved)


def body(leaf_rhs, leaf_inv, coupling, pattern, anc_rhs, anc_blocks):
    _, levels, rows, cols = anc_rhs.shape
    leaf_vb, solved, inv_t = solve(
        leaf_rhs, leaf_inv, coupling.transpose(1, 0, 2), pattern.T, anc_rhs[0], anc_blocks[0]
    )
    leaf_vb = pltpu.with_memory_space_constraint(leaf_vb, pltpu.VMEM)
    solved = pltpu.with_memory_space_constraint(solved, pltpu.VMEM)
    inv_t = pltpu.with_memory_space_constraint(inv_t, pltpu.VMEM)
    x_leaf, x_anc = tail(inv_t, leaf_vb, solved)
    return (x_leaf, x_anc.reshape(1, levels, rows, cols))


def solution(mesh):
    placed = (
        P(("layer", "row"), None),
        P(("layer", "row"), None, None),
        P(("layer", "row"), None, None),
        P(("layer", "row"), None),
        P("layer", None, "row", None),
        P("layer", None, "row", None),
    )
    return jax.shard_map(
        body,
        mesh=mesh,
        in_specs=placed,
        out_specs=(P(("layer", "row"), None), P("layer", None, "row", None)),
        check_vma=False,
    )
```

```python
import functools

import jax
import jax.numpy as jnp
from jax import lax
from jax.experimental import pallas as pl
from jax.experimental.pallas import tpu as pltpu
from jax.sharding import PartitionSpec as P

MESH = pl.DeviceIdType.MESH
LANES = 128
PIECES = 4
VMEM_BYTES = 56 * 2**20
PARTS = 8
BF, F32 = jnp.bfloat16, jnp.float32


def block_start(tree_level, level_total):
    return tree_level * level_total - tree_level * (tree_level - 1) // 2


def plan(levels, cols):
    counts, splits, count = [], [], cols // LANES
    for _ in range(levels):
        split = count % 2 == 0
        count = count // 2 if split else count
        counts.append(count)
        splits.append(split)
    return counts, splits


def tdot(a, b):
    return lax.dot_general(a, b, (((0,), (0,)), ((), ())), preferred_element_type=F32)


def dot(a, b):
    return jnp.dot(a, b, preferred_element_type=F32)


def dot_t(a, b):
    return lax.dot_general(a, b, (((1,), (1,)), ((), ())), preferred_element_type=F32)


class Copies:
    def __init__(self, send, recv):
        self.send, self.recv, self.count, self.all = send, recv, 0, []

    def start(self, src, dst, device):
        copy = pltpu.make_async_remote_copy(
            src_ref=src,
            dst_ref=dst,
            send_sem=self.send.at[self.count],
            recv_sem=self.recv.at[self.count],
            device_id=device,
            device_id_type=MESH,
        )
        copy.start()
        self.count += 1
        self.all.append(copy)
        return copy


def copies_needed(levels, n_row, counts):
    half = n_row // 2
    total = 2 * (1 + 4 * PIECES * (half - 1)) + 8 * n_row + 2 * half
    for t in range(levels - 2):
        total += counts[t] * (2 * (levels - t) + 1 + 2 * (half - 1) + half + half - 1)
    return total


def kernel(dims, rhs_in, inv_in, coup_in, pat, ancr_in, anc_in, leaf_out, out, inv_t, *scratch):
    levels, n_row, blocks, supers, width = dims
    rhs, inv, coup, ancr, anc, ly, yb, mk, mt, atr, pend, wide = scratch[:12]
    full, pair, xt, zr, kt, tt, rt, st, wr, zx, yx, pf, px, qx, tt2, yt = scratch[12:28]
    used = 28
    mid, top = levels - 2, levels - 1
    groups = []
    for _ in range(8):
        groups.append(scratch[used : used + mid])
        used += mid
    tx, rx, zs, acc, ps, pr, qs, qr = groups
    send, recv, local = scratch[used:]
    counts, splits = plan(levels, blocks * LANES)
    rows = anc.shape[1]
    half = n_row // 2
    strip = LANES // n_row
    early = block_start(mid, levels)
    lay = lax.axis_index("layer")
    row = lax.axis_index("row")
    core = lax.rem(row, 2)
    yy = row // 2
    mate = {"row": yy * 2 + (1 - core)}
    bits = [lax.rem(lay // 2**t, 2) for t in range(levels)]
    across = [{"layer": lay + (1 - 2 * bits[t]) * 2**t} for t in range(levels)]

    def slab(r, part=0, parts=1):
        size = rows // parts
        return pl.ds(pl.multiple_of(r * rows + part * size, size), size)

    loads = {}

    def load(name, src, dst):
        loads[name] = pltpu.make_async_copy(src, dst, local.at[len(loads)])
        loads[name].start()

    load("rhs", rhs_in, rhs)
    load("inv", inv_in, inv)
    load("cross", anc_in.at[early + 1], full.at[0, slab(row)])
    for s in range(levels):
        load(("coup", s), coup_in.at[s], coup.at[s])
        load(("ancr", s), ancr_in.at[s], ancr.at[s])
    load("top", anc_in.at[early + 2], full.at[1, slab(row)])
    load("anc", anc_in.at[pl.ds(0, early)], anc)
    load("mid", anc_in.at[early], pair.at[slab(core)])

    barrier = pltpu.get_barrier_semaphore()
    peers = [{"row": lax.rem(row + i, n_row)} for i in range(n_row)]
    friends = [{**across[mid], **peer} for peer in peers]
    greet = peers[1:] + friends[1:] + across
    for other in greet:
        pl.semaphore_signal(barrier, inc=1, device_id=other, device_id_type=MESH)
    copies = Copies(send, recv)

    spread = {}
    way = [mid, 0]

    def sender(i):
        return lax.rem(yy - i + half, half) * 2 + core

    def push(key, k, where, device):
        spot = full.at[k, where]
        spread[key] = copies.start(spot, spot, device)

    def piece_of(r, k, q, mine):
        h = bits[way[k]] if mine else 1 - bits[way[k]]
        return slab(r, PIECES * h + q, 2 * PIECES)

    def spread_first(k, q):
        def push_own(key, where_from, where_to, device):
            spread[key] = copies.start(
                anc_in.at[early + 1 + k, where_from], full.at[k, where_to], device
            )

        h = bits[way[k]]
        size = rows // (2 * PIECES)
        src = pl.ds(pl.multiple_of((PIECES * h + q) * size, size), size)
        for i in range(1, half):
            other = {"row": lax.rem(yy + i, half) * 2 + core}
            push_own((k, q, "y", i), src, piece_of(row, k, q, True), other)
        if q == 0:
            push_own((k, "own"), pl.ds(0, rows), slab(row), mate)

    def spread_next(k, q):
        for i in range(1, half):
            spread[k, q, "y", i].wait_recv()
            where = piece_of(sender(i), k, q, True)
            push((k, q, "far", i), k, where, across[way[k]])
            push((k, q, "mate", i), k, where, mate)

    def spread_last(k, q):
        for i in range(1, half):
            spread[k, q, "far", i].wait_recv()
            push((k, q, "mate2", i), k, piece_of(sender(i), k, q, False), mate)

    def spread_done(k):
        spread[k, "own"].wait_recv()
        for q in range(PIECES):
            for i in range(1, half):
                spread[k, q, "mate", i].wait_recv()
                spread[k, q, "mate2", i].wait_recv()

    order = list(range(counts[-1]))
    for t in reversed(range(levels)):
        if splits[t]:
            near = [bits[t] * counts[t] + j for j in order]
            order = [(1 - bits[t]) * counts[t] + j for j in order] + near
    columns = [pl.ds(pl.multiple_of(j * LANES, LANES), LANES) for j in order]

    def own(t):
        return list(range(blocks - counts[t], blocks))

    def theirs(t, p):
        return p - counts[t] if splits[t] else p

    pl.semaphore_wait(barrier, len(greet))
    for q in range(PIECES // 2):
        spread_first(0, q)
    for q in range(PIECES // 2, PIECES):
        spread_first(0, q)
    halves = copies.start(anc_in.at[early], pair.at[slab(core)], mate)
    loads["rhs"].wait()
    loads["inv"].wait()
    for k in range(supers):
        part = slice(k * width, (k + 1) * width)
        value = dot(inv[k], rhs[part])
        ly[part] = value
        yb[part] = value.astype(BF)

    def mask(s):
        loads["coup", s].wait()
        cut = slice(s * rows, (s + 1) * rows)
        for k in range(supers):
            part = slice(k * width, (k + 1) * width)
            value = coup[s, part].astype(F32) * pat[s, k].astype(F32)
            mk[part, cut] = value.astype(BF)
            mt[s, :, part] = value.T.astype(BF)

    def share(s, where):
        if ("ancr", s) in loads:
            loads.pop(("ancr", s)).wait()
        for first in range(0, len(where), 2):
            two = where[first : first + 2]
            value = dot(mt[s], jnp.concatenate([yb[:, columns[p]] for p in two], axis=1))
            for n, p in enumerate(two):
                yield ancr[s, :, columns[p]] - value[:, n * LANES : (n + 1) * LANES]

    flight = {}

    def offer_urgent(t, p, value):
        n = p - (blocks - counts[t])
        tx[t][n, 0] = value.astype(BF)
        one = pl.ds(0, 1)
        flight[t, p, 0] = copies.start(tx[t].at[n, one], rx[t].at[n, one], across[t])

    def offer_rest(t, p, values):
        n = p - (blocks - counts[t])
        for k, value in enumerate(values):
            tx[t][n, 1 + k] = value.astype(BF)
            one = pl.ds(1 + k, 1)
            flight[t, p, 1 + k] = copies.start(tx[t].at[n, one], rx[t].at[n, one], across[t])

    mask(0)
    mine = own(0)
    away = [theirs(0, p) for p in mine]
    first_shares = list(share(0, away))
    for p, value in zip(mine, first_shares):
        offer_urgent(0, p, value)
    for p, value in zip(mine, share(0, mine)):
        pend[0, p] = value
    for s in range(1, levels):
        mask(s)
    later_shares = [list(share(s, away)) for s in range(1, levels)]
    for n, p in enumerate(mine):
        offer_rest(0, p, [values[n] for values in later_shares])
    for s in range(1, levels):
        for p, value in zip(mine, share(s, mine)):
            pend[s, p] = value
    loads["anc"].wait()
    for q in range(PIECES // 2):
        spread_next(0, q)

    def turn(k):
        for other in range(n_row):
            cut = slice(other * rows, (other + 1) * rows)
            atr[k, cut] = anc[k, :, cut].T

    kept_block = own(mid)[0]
    given_block = theirs(mid, kept_block)
    near, far = {}, {}

    def hand_over(j, p):
        b = 0 if p == kept_block else 1
        xt[b, j] = pend[mid + j, p].T.astype(BF)

        def piece(i):
            return xt.at[b, j, pl.ds(pl.multiple_of(peers[i]["row"] * strip, strip), strip)]

        if p == given_block:
            for i in range(n_row):
                far[j, i] = copies.start(piece(i), zr.at[1, j, :, slab(row)], friends[i])
        if p == kept_block:
            for i in range(1, n_row):
                near[j, i] = copies.start(piece(i), zr.at[0, j, :, slab(row)], peers[i])
            zr[0, j, :, slab(row)] = piece(0)[...]

    later_work = None
    for t in range(mid):
        first_block = block_start(t, levels)
        above = levels - t - 1
        if later_work is not None:
            later_work()
        gathers, to_mate = {}, {}
        for p in own(t):
            n = p - (blocks - counts[t])
            flight[t, p, 0].wait_recv()
            zs[t][n, row] = (pend[t, p] + rx[t][n, 0].astype(F32)).astype(BF)
            spot = zs[t].at[n, row]
            for i in range(1, half):
                other = lax.rem(yy + i, half) * 2 + core
                gathers[p, i] = copies.start(spot, spot, {"row": other})
            to_mate[p] = copies.start(spot, spot, mate)
        for s in range(t + 1, levels):
            turn(first_block + s - t)
        if t == 0:
            for q in range(PIECES // 2, PIECES):
                spread_next(0, q)
            for q in range(3):
                spread_first(1, q)
        for p in own(t):
            n = p - (blocks - counts[t])

            def sums_of(slot, n=n):
                cut = pl.ds(pl.multiple_of(slot * rows, LANES), rows)
                return [
                    dot(anc[first_block + k, :, cut], zs[t][n, slot]) for k in range(1, above + 1)
                ]

            def add(old, new):
                return [a + b for a, b in zip(old, new)]

            total = sums_of(row)
            to_mate[p].wait_recv()
            total = add(total, sums_of(yy * 2 + 1 - core))
            passed = {}
            for i in range(1, half):
                gathers[p, i].wait_recv()
                origin = lax.rem(yy - i + half, half) * 2
                spot = zs[t].at[n, origin + core]
                passed[i] = copies.start(spot, spot, mate)
                total = add(total, sums_of(origin + core))
            for i in range(1, half):
                passed[i].wait_recv()
                origin = lax.rem(yy - i + half, half) * 2
                total = add(total, sums_of(origin + 1 - core))
            for k in range(above):
                flight[t, p, 1 + k].wait_recv()
                pend[t + 1 + k, p] = pend[t + 1 + k, p] + rx[t][n, 1 + k].astype(F32) - total[k]
                if t + 1 == mid:
                    hand_over(k, p)
            if t + 1 < mid:
                for q in own(t + 1):
                    if theirs(t + 1, q) == p:
                        offer_urgent(t + 1, q, pend[t + 1, p])
                        offer_rest(t + 1, q, [pend[s, p] for s in range(t + 2, levels)])

        def later_work(t=t, first_block=first_block):
            z_all = jnp.concatenate(
                [zs[t][n].reshape(n_row * rows, LANES) for n in range(counts[t])], axis=1
            )
            y_here = dot(anc[first_block], z_all).astype(BF)
            for other in range(n_row):
                acc[t][other] = tdot(anc[first_block, :, other * rows : (other + 1) * rows], y_here)

    for q in range(3, PIECES):
        spread_first(1, q)
    later_work()
    for k in range(supers):
        inv_t[k] = inv[k].T
    for q in range(PIECES // 2):
        spread_last(0, q)
    for q in range(PIECES // 2, PIECES):
        spread_last(0, q)
    for name in ("cross", "top", "mid"):
        loads[name].wait()
    halves.wait_recv()
    for q in range(3):
        spread_next(1, q)

    def gathered(j):
        for i in range(1, n_row):
            near[j, i].wait_recv()
        for i in range(n_row):
            far[j, i].wait_recv()
        return zr[0, j].astype(F32) + zr[1, j].astype(F32)

    cuts = [slice(0, half * rows), slice(half * rows, n_row * rows)]
    z_mid = gathered(0).astype(BF)
    zx[yy] = z_mid
    asked = [
        copies.start(zx.at[yy], zx.at[yy], {"row": lax.rem(yy + i, half) * 2 + core})
        for i in range(1, half)
    ]
    spread_done(0)
    mixed = gathered(1)
    last = []
    for cut in cuts:
        kt[:, cut] = mixed[:, cut] - dot_t(z_mid, full[0, cut])
        tt[:, cut] = kt[:, cut].astype(BF)
        last.append(copies.start(tt.at[:, cut], rt.at[:, cut], across[top]))
    for q in range(3, PIECES):
        spread_next(1, q)
    for q in range(PIECES // 2):
        spread_last(1, q)
    for copy in asked:
        copy.wait_recv()
    tall = n_row * rows
    yx[...] = dot_t(zx[...].reshape(half * strip, tall), pair[...]).astype(BF)
    pf[...] = dot(yx[...], pair[...]).reshape(half, strip, tall)
    px[...] = pf[...].astype(BF)
    told = []
    for i in range(1, half):
        other = lax.rem(yy + i, half)
        told.append(copies.start(px.at[other], qx.at[yy], {"row": other * 2 + core}))
    for q in range(PIECES // 2, PIECES):
        spread_last(1, q)
    spread_done(1)
    for side, copy in enumerate(last):
        copy.wait_recv()
        cut = cuts[side]
        tt2[:, cut] = (kt[:, cut] + rt[:, cut].astype(F32)).astype(BF)
        for r in range(side * half, (side + 1) * half):
            part = slice(r * rows, (r + 1) * rows)
            reach = slice(0, (r + 1) * rows)
            yt[:, part] = dot_t(tt2[:, reach], full[1, part, reach]).astype(BF)
    back = {}

    def give_back(j):
        here = pl.ds(pl.multiple_of(row * strip, strip), strip)
        sides = [peers, friends] if splits[mid] else [peers]
        for side, group in enumerate(sides):
            for i in range(1 - side, n_row):
                part = st.at[j, :, slab(peers[i]["row"])]
                back[j, side, i] = copies.start(part, wr.at[j, side, here], group[i])
        wr[j, 0, here] = st[j, :, slab(row)]

    def take_back(j):
        for side, p in ((0, kept_block), (1, given_block)):
            if side == 0 or splits[mid]:
                for i in range(1 - side, n_row):
                    back[j, side, i].wait_recv()
                wide[mid + j, p] = wr[j, side].T

    for r in range(n_row):
        part = slice(r * rows, (r + 1) * rows)
        below = slice(r * rows, n_row * rows)
        st[1, :, part] = dot(yt[:, below], full[1, below, part]).astype(BF)
    give_back(1)
    value = pf[yy] - dot(st[1], full[0])
    for copy in told:
        copy.wait_recv()
    for i in range(1, half):
        value = value + qx[lax.rem(yy + i, half)].astype(F32)
    st[0] = value.astype(BF)
    give_back(0)
    arriving = {}

    def need(s, p):
        copy = arriving.pop((s, p), None)
        if copy is not None:
            copy.wait_recv()

    def widen(s, p, t):
        if splits[t]:
            arriving[s, p - counts[t]] = copies.start(
                wide.at[s, p], wide.at[s, p - counts[t]], across[t]
            )

    def leaf_back(first, last, p):
        terms = jnp.concatenate([wide[s, p] for s in range(first, last)], axis=0)
        return ly[:, columns[p]] - dot(mk[:, first * rows : last * rows], terms)

    for j in (1, 0):
        take_back(j)
        for p in own(mid - 1):
            widen(mid + j, p, mid - 1)

    ring = list(range(1, half)) + [0]
    for t in reversed(range(mid)):
        first_block = block_start(t, levels)
        second, kept, first = {}, {}, {}

        def part_of(dest, p):
            cut = pl.ds(pl.multiple_of(dest * rows, LANES), rows)
            n = p - (blocks - counts[t])
            value = acc[t][dest, :, n * LANES : (n + 1) * LANES]
            for s in range(t + 1, levels):
                value = value - dot(atr[first_block + s - t, cut], wide[s, p])
            return value

        for p in reversed(own(t)):
            n = p - (blocks - counts[t])
            for s in range(t + 1, levels):
                need(s, p)
            for i in ring:
                dest = lax.rem(yy + i, half) * 2 + 1 - core
                ps[t][n, i] = part_of(dest, p).astype(BF)
                first[p, i] = copies.start(ps[t].at[n, i], pr[t].at[n, i], mate)
        for p in reversed(own(t)):
            n = p - (blocks - counts[t])
            for i in ring[:-1]:
                dest = lax.rem(yy + i, half) * 2 + core
                value = part_of(dest, p)
                first[p, i].wait_recv()
                qs[t][n, i - 1] = (value + pr[t][n, i].astype(F32)).astype(BF)
                second[p, i] = copies.start(
                    qs[t].at[n, i - 1], qr[t].at[n, i - 1], {"row": dest}
                )
        for p in reversed(own(t)):
            n = p - (blocks - counts[t])
            for s in range(t + 1, levels if t + 1 < mid else mid):
                widen(s, p, t)
            value = part_of(row, p)
            first[p, 0].wait_recv()
            kept[p] = value + pr[t][n, 0].astype(F32)
        if t == 0:
            for p in reversed(own(t)[1:]):
                ly[:, columns[p]] = leaf_back(1, levels, p)
        for p in reversed(own(t)):
            n = p - (blocks - counts[t])
            value = kept[p]
            for i in ring[:-1]:
                second[p, i].wait_recv()
                value = value + qr[t][n, i - 1].astype(F32)
            wide[t, p] = value.astype(BF)
            widen(t, p, t)
            if t == 0 and levels > 1 and p == own(t)[-1]:
                ly[:, columns[own(t)[0]]] = leaf_back(1, levels, own(t)[0])
    for p in reversed(own(0)):
        leaf_out[:, columns[p]] = leaf_back(0, 1, p).astype(BF)
    for p in reversed(range(blocks - counts[0])):
        for s in range(1, levels):
            need(s, p)
        if levels > 1:
            ly[:, columns[p]] = leaf_back(1, levels, p)
    for s in range(levels):
        for p in own(0):
            out[s * rows : (s + 1) * rows, columns[p]] = wide[s, p]
    for p in reversed(range(blocks - counts[0])):
        need(0, p)
        leaf_out[:, columns[p]] = leaf_back(0, 1, p).astype(BF)
        for s in range(levels):
            out[s * rows : (s + 1) * rows, columns[p]] = wide[s, p]
    for copy in copies.all:
        copy.wait_send()


def solve(leaf_rhs, leaf_inv, coupling, pattern, anc_rhs, anc):
    levels, rows, cols = anc_rhs.shape
    leaf_rows = leaf_rhs.shape[0]
    supers, width = leaf_inv.shape[:2]
    n_row = lax.axis_size("row")
    half = n_row // 2
    blocks = cols // LANES
    counts, splits = plan(levels, cols)
    span = range(levels - 2)
    early = block_start(levels - 2, levels)
    strip, tall = LANES // n_row, n_row * rows
    less = max(half - 1, 1)
    scratch = [
        pltpu.VMEM(leaf_rhs.shape, BF),
        pltpu.VMEM(leaf_inv.shape, BF),
        pltpu.VMEM(coupling.shape, BF),
        pltpu.VMEM(anc_rhs.shape, F32),
        pltpu.VMEM((early,) + anc.shape[1:], BF),
        pltpu.VMEM((leaf_rows, cols), F32),
        pltpu.VMEM((leaf_rows, cols), BF),
        pltpu.VMEM((leaf_rows, levels * rows), BF),
        pltpu.VMEM((levels, rows, leaf_rows), BF),
        pltpu.VMEM((early, n_row * rows, rows), BF),
        pltpu.VMEM((levels, blocks, rows, LANES), F32),
        pltpu.VMEM((levels, blocks, rows, LANES), BF),
    ]
    scratch += [
        pltpu.VMEM((2, tall, tall), BF),
        pltpu.VMEM((2 * rows, tall), BF),
        pltpu.VMEM((2, 2, LANES, rows), BF),
        pltpu.VMEM((2, 2, strip, tall), BF),
        pltpu.VMEM((strip, tall), F32),
        pltpu.VMEM((strip, tall), BF),
        pltpu.VMEM((strip, tall), BF),
        pltpu.VMEM((2, strip, tall), BF),
        pltpu.VMEM((2, 2, LANES, rows), BF),
        pltpu.VMEM((half, strip, tall), BF),
        pltpu.VMEM((half * strip, 2 * rows), BF),
        pltpu.VMEM((half, strip, tall), F32),
        pltpu.VMEM((half, strip, tall), BF),
        pltpu.VMEM((half, strip, tall), BF),
        pltpu.VMEM((strip, tall), BF),
        pltpu.VMEM((strip, tall), BF),
    ]
    scratch += [pltpu.VMEM((counts[t], levels - t, rows, LANES), BF) for t in span]
    scratch += [pltpu.VMEM((counts[t], levels - t, rows, LANES), BF) for t in span]
    scratch += [pltpu.VMEM((counts[t], n_row, rows, LANES), BF) for t in span]
    scratch += [pltpu.VMEM((n_row, rows, counts[t] * LANES), F32) for t in span]
    scratch += [pltpu.VMEM((counts[t], half, rows, LANES), BF) for t in span]
    scratch += [pltpu.VMEM((counts[t], half, rows, LANES), BF) for t in span]
    scratch += [pltpu.VMEM((counts[t], less, rows, LANES), BF) for t in span]
    scratch += [pltpu.VMEM((counts[t], less, rows, LANES), BF) for t in span]
    total = copies_needed(levels, n_row, counts)
    scratch += [pltpu.SemaphoreType.DMA((total,)), pltpu.SemaphoreType.DMA((total,))]
    scratch += [pltpu.SemaphoreType.DMA((2 * levels + 6,))]
    away = pl.BlockSpec(memory_space=pl.ANY)
    return pl.pallas_call(
        functools.partial(kernel, (levels, n_row, blocks, supers, width)),
        out_shape=(
            pltpu.VMEM((leaf_rows, cols), BF),
            pltpu.VMEM((levels * rows, cols), BF),
            pltpu.VMEM(leaf_inv.shape, BF),
        ),
        in_specs=[away, away, away, pl.BlockSpec(memory_space=pltpu.SMEM), away, away],
        out_specs=(pl.BlockSpec(memory_space=pltpu.VMEM),) * 3,
        scratch_shapes=scratch,
        compiler_params=pltpu.CompilerParams(collective_id=0, has_side_effects=True, vmem_limit_bytes=VMEM_BYTES),
        name="solve",
    )(leaf_rhs, leaf_inv, coupling, pattern, anc_rhs, anc)


def tail_kernel(inv_t, vb, solved, x_leaf, x_anc, leaf, anc, sems):
    count, width = inv_t.shape[:2]
    size = anc.shape[0] // PARTS
    copies = []

    def finish(src, dst, part):
        copy = pltpu.make_async_copy(src.at[part], dst.at[part], sems.at[len(copies)])
        copy.start()
        copies.append(copy)

    for k in range(PARTS):
        part = pl.ds(k * size, size)
        anc[part] = solved[part].astype(F32)
        finish(anc, x_anc, part)
    for k in range(count):
        part = pl.ds(k * width, width)
        leaf[part] = dot(inv_t[k], vb[part])
        finish(leaf, x_leaf, part)
    for copy in copies:
        copy.wait()


def tail(inv_t, leaf_vb, solved):
    count = inv_t.shape[0]
    result = (
        jax.ShapeDtypeStruct(leaf_vb.shape, F32),
        jax.ShapeDtypeStruct(solved.shape, F32),
    )
    return pl.pallas_call(
        tail_kernel,
        out_shape=result,
        in_specs=[pl.BlockSpec(memory_space=pltpu.VMEM)] * 3,
        out_specs=(pl.BlockSpec(memory_space=pl.ANY),) * 2,
        scratch_shapes=[
            pltpu.VMEM(leaf_vb.shape, F32),
            pltpu.VMEM(solved.shape, F32),
            pltpu.SemaphoreType.DMA((count + PARTS,)),
        ],
        name="tail",
    )(inv_t, leaf_vb, solved)


def body(leaf_rhs, leaf_inv, coupling, pattern, anc_rhs, anc_blocks):
    _, levels, rows, cols = anc_rhs.shape
    leaf_vb, solved, inv_t = solve(
        leaf_rhs, leaf_inv, coupling.transpose(1, 0, 2), pattern.T, anc_rhs[0], anc_blocks[0]
    )
    leaf_vb = pltpu.with_memory_space_constraint(leaf_vb, pltpu.VMEM)
    solved = pltpu.with_memory_space_constraint(solved, pltpu.VMEM)
    inv_t = pltpu.with_memory_space_constraint(inv_t, pltpu.VMEM)
    x_leaf, x_anc = tail(inv_t, leaf_vb, solved)
    return (x_leaf, x_anc.reshape(1, levels, rows, cols))


def solution(mesh):
    placed = (
        P(("layer", "row"), None),
        P(("layer", "row"), None, None),
        P(("layer", "row"), None, None),
        P(("layer", "row"), None),
        P("layer", None, "row", None),
        P("layer", None, "row", None),
    )
    return jax.shard_map(
        body,
        mesh=mesh,
        in_specs=placed,
        out_specs=(P(("layer", "row"), None), P("layer", None, "row", None)),
        check_vma=False,
    )
```

```python
import functools

import jax
import jax.numpy as jnp
from jax import lax
from jax.experimental import pallas as pl
from jax.experimental.pallas import tpu as pltpu
from jax.sharding import PartitionSpec as P

MESH = pl.DeviceIdType.MESH
LANES = 128
PIECES = 4
VMEM_BYTES = 56 * 2**20
PARTS = 8
BF, F32 = jnp.bfloat16, jnp.float32


def block_start(tree_level, level_total):
    return tree_level * level_total - tree_level * (tree_level - 1) // 2


def plan(levels, cols):
    counts, splits, count = [], [], cols // LANES
    for _ in range(levels):
        split = count % 2 == 0
        count = count // 2 if split else count
        counts.append(count)
        splits.append(split)
    return counts, splits


def tdot(a, b):
    return lax.dot_general(a, b, (((0,), (0,)), ((), ())), preferred_element_type=F32)


def dot(a, b):
    return jnp.dot(a, b, preferred_element_type=F32)


def dot_t(a, b):
    return lax.dot_general(a, b, (((1,), (1,)), ((), ())), preferred_element_type=F32)


class Copies:
    def __init__(self, send, recv):
        self.send, self.recv, self.count, self.all = send, recv, 0, []

    def start(self, src, dst, device):
        copy = pltpu.make_async_remote_copy(
            src_ref=src,
            dst_ref=dst,
            send_sem=self.send.at[self.count],
            recv_sem=self.recv.at[self.count],
            device_id=device,
            device_id_type=MESH,
        )
        copy.start()
        self.count += 1
        self.all.append(copy)
        return copy


def copies_needed(levels, n_row, counts):
    half = n_row // 2
    total = 2 * (1 + 4 * PIECES * (half - 1)) + 8 * n_row + 2 * half
    for t in range(levels - 2):
        total += counts[t] * (2 * (levels - t) + 1 + 2 * (half - 1) + half + half - 1)
    return total


def kernel(dims, rhs_in, inv_in, coup_in, pat, ancr_in, anc_in, leaf_out, out, inv_t, *scratch):
    levels, n_row, blocks, supers, width = dims
    rhs, inv, coup, ancr, anc, ly, yb, mk, mt, atr, pend, wide = scratch[:12]
    full, pair, xt, zr, kt, tt, rt, st, wr, zx, yx, pf, px, qx, tt2, yt = scratch[12:28]
    used = 28
    mid, top = levels - 2, levels - 1
    groups = []
    for _ in range(8):
        groups.append(scratch[used : used + mid])
        used += mid
    tx, rx, zs, acc, ps, pr, qs, qr = groups
    send, recv, local = scratch[used:]
    counts, splits = plan(levels, blocks * LANES)
    rows = anc.shape[1]
    half = n_row // 2
    strip = LANES // n_row
    early = block_start(mid, levels)
    lay = lax.axis_index("layer")
    row = lax.axis_index("row")
    core = lax.rem(row, 2)
    yy = row // 2
    mate = {"row": yy * 2 + (1 - core)}
    bits = [lax.rem(lay // 2**t, 2) for t in range(levels)]
    across = [{"layer": lay + (1 - 2 * bits[t]) * 2**t} for t in range(levels)]

    def slab(r, part=0, parts=1):
        size = rows // parts
        return pl.ds(pl.multiple_of(r * rows + part * size, size), size)

    loads = {}

    def load(name, src, dst):
        loads[name] = pltpu.make_async_copy(src, dst, local.at[len(loads)])
        loads[name].start()

    load("rhs", rhs_in, rhs)
    load("inv", inv_in, inv)
    load("cross", anc_in.at[early + 1], full.at[0, slab(row)])
    for s in range(levels):
        load(("coup", s), coup_in.at[s], coup.at[s])
        load(("ancr", s), ancr_in.at[s], ancr.at[s])
    load("top", anc_in.at[early + 2], full.at[1, slab(row)])
    load("anc", anc_in.at[pl.ds(0, early)], anc)
    load("mid", anc_in.at[early], pair.at[slab(core)])

    barrier = pltpu.get_barrier_semaphore()
    peers = [{"row": lax.rem(row + i, n_row)} for i in range(n_row)]
    friends = [{**across[mid], **peer} for peer in peers]
    greet = peers[1:] + friends[1:] + across
    for other in greet:
        pl.semaphore_signal(barrier, inc=1, device_id=other, device_id_type=MESH)
    copies = Copies(send, recv)

    spread = {}
    way = [mid, 0]

    def sender(i):
        return lax.rem(yy - i + half, half) * 2 + core

    def push(key, k, where, device):
        spot = full.at[k, where]
        spread[key] = copies.start(spot, spot, device)

    def piece_of(r, k, q, mine):
        h = bits[way[k]] if mine else 1 - bits[way[k]]
        return slab(r, PIECES * h + q, 2 * PIECES)

    def spread_first(k, q):
        def push_own(key, where_from, where_to, device):
            spread[key] = copies.start(
                anc_in.at[early + 1 + k, where_from], full.at[k, where_to], device
            )

        h = bits[way[k]]
        size = rows // (2 * PIECES)
        src = pl.ds(pl.multiple_of((PIECES * h + q) * size, size), size)
        for i in range(1, half):
            other = {"row": lax.rem(yy + i, half) * 2 + core}
            push_own((k, q, "y", i), src, piece_of(row, k, q, True), other)
        if q == 0:
            push_own((k, "own"), pl.ds(0, rows), slab(row), mate)

    def spread_next(k, q):
        for i in range(1, half):
            spread[k, q, "y", i].wait_recv()
            where = piece_of(sender(i), k, q, True)
            push((k, q, "far", i), k, where, across[way[k]])
            push((k, q, "mate", i), k, where, mate)

    def spread_last(k, q):
        for i in range(1, half):
            spread[k, q, "far", i].wait_recv()
            push((k, q, "mate2", i), k, piece_of(sender(i), k, q, False), mate)

    def spread_done(k):
        spread[k, "own"].wait_recv()
        for q in range(PIECES):
            for i in range(1, half):
                spread[k, q, "mate", i].wait_recv()
                spread[k, q, "mate2", i].wait_recv()

    order = list(range(counts[-1]))
    for t in reversed(range(levels)):
        if splits[t]:
            near = [bits[t] * counts[t] + j for j in order]
            order = [(1 - bits[t]) * counts[t] + j for j in order] + near
    columns = [pl.ds(pl.multiple_of(j * LANES, LANES), LANES) for j in order]

    def own(t):
        return list(range(blocks - counts[t], blocks))

    def theirs(t, p):
        return p - counts[t] if splits[t] else p

    pl.semaphore_wait(barrier, len(greet))
    for q in range(PIECES // 2):
        spread_first(0, q)
    for q in range(PIECES // 2, PIECES):
        spread_first(0, q)
    halves = copies.start(anc_in.at[early], pair.at[slab(core)], mate)
    loads["rhs"].wait()
    loads["inv"].wait()
    for k in range(supers):
        part = slice(k * width, (k + 1) * width)
        value = dot(inv[k], rhs[part])
        ly[part] = value
        yb[part] = value.astype(BF)

    def mask(s):
        loads["coup", s].wait()
        cut = slice(s * rows, (s + 1) * rows)
        for k in range(supers):
            part = slice(k * width, (k + 1) * width)
            value = coup[s, part].astype(F32) * pat[s, k].astype(F32)
            mk[part, cut] = value.astype(BF)
            mt[s, :, part] = value.T.astype(BF)

    def share(s, where):
        if ("ancr", s) in loads:
            loads.pop(("ancr", s)).wait()
        for first in range(0, len(where), 2):
            two = where[first : first + 2]
            value = dot(mt[s], jnp.concatenate([yb[:, columns[p]] for p in two], axis=1))
            for n, p in enumerate(two):
                yield ancr[s, :, columns[p]] - value[:, n * LANES : (n + 1) * LANES]

    flight = {}

    def offer_urgent(t, p, value):
        n = p - (blocks - counts[t])
        tx[t][n, 0] = value.astype(BF)
        one = pl.ds(0, 1)
        flight[t, p, 0] = copies.start(tx[t].at[n, one], rx[t].at[n, one], across[t])

    def offer_rest(t, p, values):
        n = p - (blocks - counts[t])
        for k, value in enumerate(values):
            tx[t][n, 1 + k] = value.astype(BF)
            one = pl.ds(1 + k, 1)
            flight[t, p, 1 + k] = copies.start(tx[t].at[n, one], rx[t].at[n, one], across[t])

    mask(0)
    mine = own(0)
    away = [theirs(0, p) for p in mine]
    first_shares = list(share(0, away))
    for p, value in zip(mine, first_shares):
        offer_urgent(0, p, value)
    for p, value in zip(mine, share(0, mine)):
        pend[0, p] = value
    for s in range(1, levels):
        mask(s)
    later_shares = [list(share(s, away)) for s in range(1, levels)]
    for n, p in enumerate(mine):
        offer_rest(0, p, [values[n] for values in later_shares])
    for s in range(1, levels):
        for p, value in zip(mine, share(s, mine)):
            pend[s, p] = value
    loads["anc"].wait()
    for q in range(PIECES // 2):
        spread_next(0, q)

    def turn(k):
        for other in range(n_row):
            cut = slice(other * rows, (other + 1) * rows)
            atr[k, cut] = anc[k, :, cut].T

    kept_block = own(mid)[0]
    given_block = theirs(mid, kept_block)
    near, far = {}, {}

    def hand_over(j, p):
        b = 0 if p == kept_block else 1
        xt[b, j] = pend[mid + j, p].T.astype(BF)

        def piece(i):
            return xt.at[b, j, pl.ds(pl.multiple_of(peers[i]["row"] * strip, strip), strip)]

        if p == given_block:
            for i in range(n_row):
                far[j, i] = copies.start(piece(i), zr.at[1, j, :, slab(row)], friends[i])
        if p == kept_block:
            for i in range(1, n_row):
                near[j, i] = copies.start(piece(i), zr.at[0, j, :, slab(row)], peers[i])
            zr[0, j, :, slab(row)] = piece(0)[...]

    later_work = None
    for t in range(mid):
        first_block = block_start(t, levels)
        above = levels - t - 1
        if later_work is not None:
            later_work()
        gathers, to_mate = {}, {}
        for p in own(t):
            n = p - (blocks - counts[t])
            flight[t, p, 0].wait_recv()
            zs[t][n, row] = (pend[t, p] + rx[t][n, 0].astype(F32)).astype(BF)
            spot = zs[t].at[n, row]
            for i in range(1, half):
                other = lax.rem(yy + i, half) * 2 + core
                gathers[p, i] = copies.start(spot, spot, {"row": other})
            to_mate[p] = copies.start(spot, spot, mate)
        for s in range(t + 1, levels):
            turn(first_block + s - t)
        if t == 0:
            for q in range(PIECES // 2, PIECES):
                spread_next(0, q)
            for q in range(3):
                spread_first(1, q)
        for p in own(t):
            n = p - (blocks - counts[t])

            def sums_of(slot, n=n):
                cut = pl.ds(pl.multiple_of(slot * rows, LANES), rows)
                return [
                    dot(anc[first_block + k, :, cut], zs[t][n, slot]) for k in range(1, above + 1)
                ]

            def add(old, new):
                return [a + b for a, b in zip(old, new)]

            total = sums_of(row)
            to_mate[p].wait_recv()
            total = add(total, sums_of(yy * 2 + 1 - core))
            passed = {}
            for i in range(1, half):
                gathers[p, i].wait_recv()
                origin = lax.rem(yy - i + half, half) * 2
                spot = zs[t].at[n, origin + core]
                passed[i] = copies.start(spot, spot, mate)
                total = add(total, sums_of(origin + core))
            for i in range(1, half):
                passed[i].wait_recv()
                origin = lax.rem(yy - i + half, half) * 2
                total = add(total, sums_of(origin + 1 - core))
            for k in range(above):
                flight[t, p, 1 + k].wait_recv()
                pend[t + 1 + k, p] = pend[t + 1 + k, p] + rx[t][n, 1 + k].astype(F32) - total[k]
                if t + 1 == mid:
                    hand_over(k, p)
            if t + 1 < mid:
                for q in own(t + 1):
                    if theirs(t + 1, q) == p:
                        offer_urgent(t + 1, q, pend[t + 1, p])
                        offer_rest(t + 1, q, [pend[s, p] for s in range(t + 2, levels)])

        def later_work(t=t, first_block=first_block):
            z_all = jnp.concatenate(
                [zs[t][n].reshape(n_row * rows, LANES) for n in range(counts[t])], axis=1
            )
            y_here = dot(anc[first_block], z_all).astype(BF)
            for other in range(n_row):
                acc[t][other] = tdot(anc[first_block, :, other * rows : (other + 1) * rows], y_here)

    for q in range(3, PIECES):
        spread_first(1, q)
    later_work()
    for k in range(supers):
        inv_t[k] = inv[k].T
    for q in range(PIECES // 2):
        spread_last(0, q)
    for q in range(PIECES // 2, PIECES):
        spread_last(0, q)
    for name in ("cross", "top", "mid"):
        loads[name].wait()
    halves.wait_recv()
    for q in range(3):
        spread_next(1, q)

    def gathered(j):
        for i in range(1, n_row):
            near[j, i].wait_recv()
        for i in range(n_row):
            far[j, i].wait_recv()
        return zr[0, j].astype(F32) + zr[1, j].astype(F32)

    cuts = [slice(0, half * rows), slice(half * rows, n_row * rows)]
    z_mid = gathered(0).astype(BF)
    zx[yy] = z_mid
    asked = [
        copies.start(zx.at[yy], zx.at[yy], {"row": lax.rem(yy + i, half) * 2 + core})
        for i in range(1, half)
    ]
    spread_done(0)
    product = dot_t(z_mid, full[0, cuts[0]])
    mixed = gathered(1)
    last = []
    for cut in cuts:
        if cut is not cuts[0]:
            product = dot_t(z_mid, full[0, cut])
        kt[:, cut] = mixed[:, cut] - product
        tt[:, cut] = kt[:, cut].astype(BF)
        last.append(copies.start(tt.at[:, cut], rt.at[:, cut], across[top]))
    for q in range(3, PIECES):
        spread_next(1, q)
    for q in range(PIECES // 2):
        spread_last(1, q)
    for copy in asked:
        copy.wait_recv()
    tall = n_row * rows
    yx[...] = dot_t(zx[...].reshape(half * strip, tall), pair[...]).astype(BF)
    pf[...] = dot(yx[...], pair[...]).reshape(half, strip, tall)
    px[...] = pf[...].astype(BF)
    told = []
    for i in range(1, half):
        other = lax.rem(yy + i, half)
        told.append(copies.start(px.at[other], qx.at[yy], {"row": other * 2 + core}))
    for q in range(PIECES // 2, PIECES):
        spread_last(1, q)
    spread_done(1)
    for side, copy in enumerate(last):
        copy.wait_recv()
        cut = cuts[side]
        tt2[:, cut] = (kt[:, cut] + rt[:, cut].astype(F32)).astype(BF)
        for r in range(side * half, (side + 1) * half):
            part = slice(r * rows, (r + 1) * rows)
            reach = slice(0, (r + 1) * rows)
            yt[:, part] = dot_t(tt2[:, reach], full[1, part, reach]).astype(BF)
    back = {}

    def give_back(j):
        here = pl.ds(pl.multiple_of(row * strip, strip), strip)
        sides = [peers, friends] if splits[mid] else [peers]
        for side, group in enumerate(sides):
            for i in range(1 - side, n_row):
                part = st.at[j, :, slab(peers[i]["row"])]
                back[j, side, i] = copies.start(part, wr.at[j, side, here], group[i])
        wr[j, 0, here] = st[j, :, slab(row)]

    def take_back(j):
        for side, p in ((0, kept_block), (1, given_block)):
            if side == 0 or splits[mid]:
                for i in range(1 - side, n_row):
                    back[j, side, i].wait_recv()
                wide[mid + j, p] = wr[j, side].T

    for r in range(n_row):
        part = slice(r * rows, (r + 1) * rows)
        below = slice(r * rows, n_row * rows)
        st[1, :, part] = dot(yt[:, below], full[1, below, part]).astype(BF)
    give_back(1)
    value = pf[yy] - dot(st[1], full[0])
    for copy in told:
        copy.wait_recv()
    for i in range(1, half):
        value = value + qx[lax.rem(yy + i, half)].astype(F32)
    st[0] = value.astype(BF)
    give_back(0)
    arriving = {}

    def need(s, p):
        copy = arriving.pop((s, p), None)
        if copy is not None:
            copy.wait_recv()

    def widen(s, p, t):
        if splits[t]:
            arriving[s, p - counts[t]] = copies.start(
                wide.at[s, p], wide.at[s, p - counts[t]], across[t]
            )

    def leaf_back(first, last, p):
        terms = jnp.concatenate([wide[s, p] for s in range(first, last)], axis=0)
        return ly[:, columns[p]] - dot(mk[:, first * rows : last * rows], terms)

    for j in (1, 0):
        take_back(j)
        for p in own(mid - 1):
            widen(mid + j, p, mid - 1)

    ring = list(range(1, half)) + [0]
    for t in reversed(range(mid)):
        first_block = block_start(t, levels)
        second, kept, first = {}, {}, {}

        def part_of(dest, p):
            cut = pl.ds(pl.multiple_of(dest * rows, LANES), rows)
            n = p - (blocks - counts[t])
            value = acc[t][dest, :, n * LANES : (n + 1) * LANES]
            for s in range(t + 1, levels):
                value = value - dot(atr[first_block + s - t, cut], wide[s, p])
            return value

        for p in reversed(own(t)):
            n = p - (blocks - counts[t])
            for s in range(t + 1, levels):
                need(s, p)
            for i in ring:
                dest = lax.rem(yy + i, half) * 2 + 1 - core
                ps[t][n, i] = part_of(dest, p).astype(BF)
                first[p, i] = copies.start(ps[t].at[n, i], pr[t].at[n, i], mate)
        for p in reversed(own(t)):
            n = p - (blocks - counts[t])
            for i in ring[:-1]:
                dest = lax.rem(yy + i, half) * 2 + core
                value = part_of(dest, p)
                first[p, i].wait_recv()
                qs[t][n, i - 1] = (value + pr[t][n, i].astype(F32)).astype(BF)
                second[p, i] = copies.start(
                    qs[t].at[n, i - 1], qr[t].at[n, i - 1], {"row": dest}
                )
        for p in reversed(own(t)):
            n = p - (blocks - counts[t])
            for s in range(t + 1, levels if t + 1 < mid else mid):
                widen(s, p, t)
            value = part_of(row, p)
            first[p, 0].wait_recv()
            kept[p] = value + pr[t][n, 0].astype(F32)
        if t == 0:
            for p in reversed(own(t)[1:]):
                ly[:, columns[p]] = leaf_back(1, levels, p)
        for p in reversed(own(t)):
            n = p - (blocks - counts[t])
            value = kept[p]
            for i in ring[:-1]:
                second[p, i].wait_recv()
                value = value + qr[t][n, i - 1].astype(F32)
            wide[t, p] = value.astype(BF)
            widen(t, p, t)
            if t == 0 and levels > 1 and p == own(t)[-1]:
                ly[:, columns[own(t)[0]]] = leaf_back(1, levels, own(t)[0])
    for p in reversed(own(0)):
        leaf_out[:, columns[p]] = leaf_back(0, 1, p).astype(BF)
    for p in reversed(range(blocks - counts[0])):
        for s in range(1, levels):
            need(s, p)
        if levels > 1:
            ly[:, columns[p]] = leaf_back(1, levels, p)
    for s in range(levels):
        for p in own(0):
            out[s * rows : (s + 1) * rows, columns[p]] = wide[s, p]
    for p in reversed(range(blocks - counts[0])):
        need(0, p)
        leaf_out[:, columns[p]] = leaf_back(0, 1, p).astype(BF)
        for s in range(levels):
            out[s * rows : (s + 1) * rows, columns[p]] = wide[s, p]
    for copy in copies.all:
        copy.wait_send()


def solve(leaf_rhs, leaf_inv, coupling, pattern, anc_rhs, anc):
    levels, rows, cols = anc_rhs.shape
    leaf_rows = leaf_rhs.shape[0]
    supers, width = leaf_inv.shape[:2]
    n_row = lax.axis_size("row")
    half = n_row // 2
    blocks = cols // LANES
    counts, splits = plan(levels, cols)
    span = range(levels - 2)
    early = block_start(levels - 2, levels)
    strip, tall = LANES // n_row, n_row * rows
    less = max(half - 1, 1)
    scratch = [
        pltpu.VMEM(leaf_rhs.shape, BF),
        pltpu.VMEM(leaf_inv.shape, BF),
        pltpu.VMEM(coupling.shape, BF),
        pltpu.VMEM(anc_rhs.shape, F32),
        pltpu.VMEM((early,) + anc.shape[1:], BF),
        pltpu.VMEM((leaf_rows, cols), F32),
        pltpu.VMEM((leaf_rows, cols), BF),
        pltpu.VMEM((leaf_rows, levels * rows), BF),
        pltpu.VMEM((levels, rows, leaf_rows), BF),
        pltpu.VMEM((early, n_row * rows, rows), BF),
        pltpu.VMEM((levels, blocks, rows, LANES), F32),
        pltpu.VMEM((levels, blocks, rows, LANES), BF),
    ]
    scratch += [
        pltpu.VMEM((2, tall, tall), BF),
        pltpu.VMEM((2 * rows, tall), BF),
        pltpu.VMEM((2, 2, LANES, rows), BF),
        pltpu.VMEM((2, 2, strip, tall), BF),
        pltpu.VMEM((strip, tall), F32),
        pltpu.VMEM((strip, tall), BF),
        pltpu.VMEM((strip, tall), BF),
        pltpu.VMEM((2, strip, tall), BF),
        pltpu.VMEM((2, 2, LANES, rows), BF),
        pltpu.VMEM((half, strip, tall), BF),
        pltpu.VMEM((half * strip, 2 * rows), BF),
        pltpu.VMEM((half, strip, tall), F32),
        pltpu.VMEM((half, strip, tall), BF),
        pltpu.VMEM((half, strip, tall), BF),
        pltpu.VMEM((strip, tall), BF),
        pltpu.VMEM((strip, tall), BF),
    ]
    scratch += [pltpu.VMEM((counts[t], levels - t, rows, LANES), BF) for t in span]
    scratch += [pltpu.VMEM((counts[t], levels - t, rows, LANES), BF) for t in span]
    scratch += [pltpu.VMEM((counts[t], n_row, rows, LANES), BF) for t in span]
    scratch += [pltpu.VMEM((n_row, rows, counts[t] * LANES), F32) for t in span]
    scratch += [pltpu.VMEM((counts[t], half, rows, LANES), BF) for t in span]
    scratch += [pltpu.VMEM((counts[t], half, rows, LANES), BF) for t in span]
    scratch += [pltpu.VMEM((counts[t], less, rows, LANES), BF) for t in span]
    scratch += [pltpu.VMEM((counts[t], less, rows, LANES), BF) for t in span]
    total = copies_needed(levels, n_row, counts)
    scratch += [pltpu.SemaphoreType.DMA((total,)), pltpu.SemaphoreType.DMA((total,))]
    scratch += [pltpu.SemaphoreType.DMA((2 * levels + 6,))]
    away = pl.BlockSpec(memory_space=pl.ANY)
    return pl.pallas_call(
        functools.partial(kernel, (levels, n_row, blocks, supers, width)),
        out_shape=(
            pltpu.VMEM((leaf_rows, cols), BF),
            pltpu.VMEM((levels * rows, cols), BF),
            pltpu.VMEM(leaf_inv.shape, BF),
        ),
        in_specs=[away, away, away, pl.BlockSpec(memory_space=pltpu.SMEM), away, away],
        out_specs=(pl.BlockSpec(memory_space=pltpu.VMEM),) * 3,
        scratch_shapes=scratch,
        compiler_params=pltpu.CompilerParams(collective_id=0, has_side_effects=True, vmem_limit_bytes=VMEM_BYTES),
        name="solve",
    )(leaf_rhs, leaf_inv, coupling, pattern, anc_rhs, anc)


def tail_kernel(inv_t, vb, solved, x_leaf, x_anc, leaf, anc, sems):
    count, width = inv_t.shape[:2]
    size = anc.shape[0] // PARTS
    copies = []

    def finish(src, dst, part):
        copy = pltpu.make_async_copy(src.at[part], dst.at[part], sems.at[len(copies)])
        copy.start()
        copies.append(copy)

    for k in range(PARTS):
        part = pl.ds(k * size, size)
        anc[part] = solved[part].astype(F32)
        finish(anc, x_anc, part)
    for k in range(count):
        part = pl.ds(k * width, width)
        leaf[part] = dot(inv_t[k], vb[part])
        finish(leaf, x_leaf, part)
    for copy in copies:
        copy.wait()


def tail(inv_t, leaf_vb, solved):
    count = inv_t.shape[0]
    result = (
        jax.ShapeDtypeStruct(leaf_vb.shape, F32),
        jax.ShapeDtypeStruct(solved.shape, F32),
    )
    return pl.pallas_call(
        tail_kernel,
        out_shape=result,
        in_specs=[pl.BlockSpec(memory_space=pltpu.VMEM)] * 3,
        out_specs=(pl.BlockSpec(memory_space=pl.ANY),) * 2,
        scratch_shapes=[
            pltpu.VMEM(leaf_vb.shape, F32),
            pltpu.VMEM(solved.shape, F32),
            pltpu.SemaphoreType.DMA((count + PARTS,)),
        ],
        name="tail",
    )(inv_t, leaf_vb, solved)


def body(leaf_rhs, leaf_inv, coupling, pattern, anc_rhs, anc_blocks):
    _, levels, rows, cols = anc_rhs.shape
    leaf_vb, solved, inv_t = solve(
        leaf_rhs, leaf_inv, coupling.transpose(1, 0, 2), pattern.T, anc_rhs[0], anc_blocks[0]
    )
    leaf_vb = pltpu.with_memory_space_constraint(leaf_vb, pltpu.VMEM)
    solved = pltpu.with_memory_space_constraint(solved, pltpu.VMEM)
    inv_t = pltpu.with_memory_space_constraint(inv_t, pltpu.VMEM)
    x_leaf, x_anc = tail(inv_t, leaf_vb, solved)
    return (x_leaf, x_anc.reshape(1, levels, rows, cols))


def solution(mesh):
    placed = (
        P(("layer", "row"), None),
        P(("layer", "row"), None, None),
        P(("layer", "row"), None, None),
        P(("layer", "row"), None),
        P("layer", None, "row", None),
        P("layer", None, "row", None),
    )
    return jax.shard_map(
        body,
        mesh=mesh,
        in_specs=placed,
        out_specs=(P(("layer", "row"), None), P("layer", None, "row", None)),
        check_vma=False,
    )
```

```python
import functools

import jax
import jax.numpy as jnp
from jax import lax
from jax.experimental import pallas as pl
from jax.experimental.pallas import tpu as pltpu
from jax.sharding import PartitionSpec as P

MESH = pl.DeviceIdType.MESH
LANES = 128
PIECES = 4
VMEM_BYTES = 56 * 2**20
PARTS = 8
BF, F32 = jnp.bfloat16, jnp.float32


def block_start(tree_level, level_total):
    return tree_level * level_total - tree_level * (tree_level - 1) // 2


def plan(levels, cols):
    counts, splits, count = [], [], cols // LANES
    for _ in range(levels):
        split = count % 2 == 0
        count = count // 2 if split else count
        counts.append(count)
        splits.append(split)
    return counts, splits


def tdot(a, b):
    return lax.dot_general(a, b, (((0,), (0,)), ((), ())), preferred_element_type=F32)


def dot(a, b):
    return jnp.dot(a, b, preferred_element_type=F32)


def dot_t(a, b):
    return lax.dot_general(a, b, (((1,), (1,)), ((), ())), preferred_element_type=F32)


class Copies:
    def __init__(self, send, recv):
        self.send, self.recv, self.count, self.all = send, recv, 0, []

    def start(self, src, dst, device):
        copy = pltpu.make_async_remote_copy(
            src_ref=src,
            dst_ref=dst,
            send_sem=self.send.at[self.count],
            recv_sem=self.recv.at[self.count],
            device_id=device,
            device_id_type=MESH,
        )
        copy.start()
        self.count += 1
        self.all.append(copy)
        return copy


def copies_needed(levels, n_row, counts):
    half = n_row // 2
    total = 2 * (1 + 4 * PIECES * (half - 1)) + 8 * n_row + 2 * half
    for t in range(levels - 2):
        total += counts[t] * (2 * (levels - t) + 1 + 2 * (half - 1) + half + half - 1)
    return total


def kernel(dims, rhs_in, inv_in, coup_in, pat, ancr_in, anc_in, leaf_out, out, inv_t, *scratch):
    levels, n_row, blocks, supers, width = dims
    rhs, inv, coup, ancr, anc, ly, yb, mk, mt, atr, pend, wide = scratch[:12]
    full, pair, xt, zr, kt, tt, rt, st, wr, zx, yx, pf, px, qx, tt2, yt = scratch[12:28]
    used = 28
    mid, top = levels - 2, levels - 1
    groups = []
    for _ in range(8):
        groups.append(scratch[used : used + mid])
        used += mid
    tx, rx, zs, acc, ps, pr, qs, qr = groups
    send, recv, local = scratch[used:]
    counts, splits = plan(levels, blocks * LANES)
    rows = anc.shape[1]
    half = n_row // 2
    strip = LANES // n_row
    early = block_start(mid, levels)
    lay = lax.axis_index("layer")
    row = lax.axis_index("row")
    core = lax.rem(row, 2)
    yy = row // 2
    mate = {"row": yy * 2 + (1 - core)}
    bits = [lax.rem(lay // 2**t, 2) for t in range(levels)]
    across = [{"layer": lay + (1 - 2 * bits[t]) * 2**t} for t in range(levels)]

    def slab(r, part=0, parts=1):
        size = rows // parts
        return pl.ds(pl.multiple_of(r * rows + part * size, size), size)

    loads = {}

    def load(name, src, dst):
        loads[name] = pltpu.make_async_copy(src, dst, local.at[len(loads)])
        loads[name].start()

    load("rhs", rhs_in, rhs)
    load("inv", inv_in, inv)
    load("cross", anc_in.at[early + 1], full.at[0, slab(row)])
    for s in range(levels):
        load(("coup", s), coup_in.at[s], coup.at[s])
        load(("ancr", s), ancr_in.at[s], ancr.at[s])
    load("top", anc_in.at[early + 2], full.at[1, slab(row)])
    load("anc", anc_in.at[pl.ds(0, early)], anc)
    load("mid", anc_in.at[early], pair.at[slab(core)])

    barrier = pltpu.get_barrier_semaphore()
    peers = [{"row": lax.rem(row + i, n_row)} for i in range(n_row)]
    friends = [{**across[mid], **peer} for peer in peers]
    greet = peers[1:] + friends[1:] + across
    for other in greet:
        pl.semaphore_signal(barrier, inc=1, device_id=other, device_id_type=MESH)
    copies = Copies(send, recv)

    spread = {}
    way = [mid, 0]

    def sender(i):
        return lax.rem(yy - i + half, half) * 2 + core

    def push(key, k, where, device):
        spot = full.at[k, where]
        spread[key] = copies.start(spot, spot, device)

    def piece_of(r, k, q, mine):
        h = bits[way[k]] if mine else 1 - bits[way[k]]
        return slab(r, PIECES * h + q, 2 * PIECES)

    def spread_first(k, q):
        def push_own(key, where_from, where_to, device):
            spread[key] = copies.start(
                anc_in.at[early + 1 + k, where_from], full.at[k, where_to], device
            )

        h = bits[way[k]]
        size = rows // (2 * PIECES)
        src = pl.ds(pl.multiple_of((PIECES * h + q) * size, size), size)
        for i in range(1, half):
            other = {"row": lax.rem(yy + i, half) * 2 + core}
            push_own((k, q, "y", i), src, piece_of(row, k, q, True), other)
        if q == 0:
            push_own((k, "own"), pl.ds(0, rows), slab(row), mate)

    def spread_next(k, q):
        for i in range(1, half):
            spread[k, q, "y", i].wait_recv()
            where = piece_of(sender(i), k, q, True)
            push((k, q, "far", i), k, where, across[way[k]])
            push((k, q, "mate", i), k, where, mate)

    def spread_last(k, q):
        for i in range(1, half):
            spread[k, q, "far", i].wait_recv()
            push((k, q, "mate2", i), k, piece_of(sender(i), k, q, False), mate)

    def spread_done(k):
        spread[k, "own"].wait_recv()
        for q in range(PIECES):
            for i in range(1, half):
                spread[k, q, "mate", i].wait_recv()
                spread[k, q, "mate2", i].wait_recv()

    order = list(range(counts[-1]))
    for t in reversed(range(levels)):
        if splits[t]:
            near = [bits[t] * counts[t] + j for j in order]
            order = [(1 - bits[t]) * counts[t] + j for j in order] + near
    columns = [pl.ds(pl.multiple_of(j * LANES, LANES), LANES) for j in order]

    def own(t):
        return list(range(blocks - counts[t], blocks))

    def theirs(t, p):
        return p - counts[t] if splits[t] else p

    pl.semaphore_wait(barrier, len(greet))
    for q in range(PIECES // 2):
        spread_first(0, q)
    for q in range(PIECES // 2, PIECES):
        spread_first(0, q)
    halves = copies.start(anc_in.at[early], pair.at[slab(core)], mate)
    loads["rhs"].wait()
    loads["inv"].wait()
    for k in range(supers):
        part = slice(k * width, (k + 1) * width)
        value = dot(inv[k], rhs[part])
        ly[part] = value
        yb[part] = value.astype(BF)

    def mask(s):
        loads["coup", s].wait()
        cut = slice(s * rows, (s + 1) * rows)
        for k in range(supers):
            part = slice(k * width, (k + 1) * width)
            value = coup[s, part].astype(F32) * pat[s, k].astype(F32)
            mk[part, cut] = value.astype(BF)
            mt[s, :, part] = value.T.astype(BF)

    def share(s, where):
        if ("ancr", s) in loads:
            loads.pop(("ancr", s)).wait()
        for first in range(0, len(where), 2):
            two = where[first : first + 2]
            value = dot(mt[s], jnp.concatenate([yb[:, columns[p]] for p in two], axis=1))
            for n, p in enumerate(two):
                yield ancr[s, :, columns[p]] - value[:, n * LANES : (n + 1) * LANES]

    flight = {}

    def offer_urgent(t, p, value):
        n = p - (blocks - counts[t])
        tx[t][n, 0] = value.astype(BF)
        one = pl.ds(0, 1)
        flight[t, p, 0] = copies.start(tx[t].at[n, one], rx[t].at[n, one], across[t])

    def offer_rest(t, p, values):
        n = p - (blocks - counts[t])
        for k, value in enumerate(values):
            tx[t][n, 1 + k] = value.astype(BF)
            one = pl.ds(1 + k, 1)
            flight[t, p, 1 + k] = copies.start(tx[t].at[n, one], rx[t].at[n, one], across[t])

    mask(0)
    mine = own(0)
    away = [theirs(0, p) for p in mine]
    first_shares = list(share(0, away))
    for p, value in zip(mine, first_shares):
        offer_urgent(0, p, value)
    for p, value in zip(mine, share(0, mine)):
        pend[0, p] = value
    for s in range(1, levels):
        mask(s)
    later_shares = [list(share(s, away)) for s in range(1, levels)]
    for n, p in enumerate(mine):
        offer_rest(0, p, [values[n] for values in later_shares])
    for s in range(1, levels):
        for p, value in zip(mine, share(s, mine)):
            pend[s, p] = value
    loads["anc"].wait()
    for q in range(PIECES // 2):
        spread_next(0, q)

    def turn(k):
        for other in range(n_row):
            cut = slice(other * rows, (other + 1) * rows)
            atr[k, cut] = anc[k, :, cut].T

    kept_block = own(mid)[0]
    given_block = theirs(mid, kept_block)
    near, far = {}, {}

    def hand_over(j, p):
        b = 0 if p == kept_block else 1
        xt[b, j] = pend[mid + j, p].T.astype(BF)

        def piece(i):
            return xt.at[b, j, pl.ds(pl.multiple_of(peers[i]["row"] * strip, strip), strip)]

        if p == given_block:
            for i in range(n_row):
                far[j, i] = copies.start(piece(i), zr.at[1, j, :, slab(row)], friends[i])
        if p == kept_block:
            for i in range(1, n_row):
                near[j, i] = copies.start(piece(i), zr.at[0, j, :, slab(row)], peers[i])
            zr[0, j, :, slab(row)] = piece(0)[...]

    later_work = None
    for t in range(mid):
        first_block = block_start(t, levels)
        above = levels - t - 1
        if later_work is not None:
            later_work()
        gathers, to_mate = {}, {}
        for p in own(t):
            n = p - (blocks - counts[t])
            flight[t, p, 0].wait_recv()
            zs[t][n, row] = (pend[t, p] + rx[t][n, 0].astype(F32)).astype(BF)
            spot = zs[t].at[n, row]
            for i in range(1, half):
                other = lax.rem(yy + i, half) * 2 + core
                gathers[p, i] = copies.start(spot, spot, {"row": other})
            to_mate[p] = copies.start(spot, spot, mate)
        for s in range(t + 1, levels):
            turn(first_block + s - t)
        if t == 0:
            for q in range(PIECES // 2, PIECES):
                spread_next(0, q)
            for q in range(3):
                spread_first(1, q)
        for p in own(t):
            n = p - (blocks - counts[t])

            def sums_of(slot, n=n):
                cut = pl.ds(pl.multiple_of(slot * rows, LANES), rows)
                return [
                    dot(anc[first_block + k, :, cut], zs[t][n, slot]) for k in range(1, above + 1)
                ]

            def add(old, new):
                return [a + b for a, b in zip(old, new)]

            total = sums_of(row)
            to_mate[p].wait_recv()
            total = add(total, sums_of(yy * 2 + 1 - core))
            passed = {}
            for i in range(1, half):
                gathers[p, i].wait_recv()
                origin = lax.rem(yy - i + half, half) * 2
                spot = zs[t].at[n, origin + core]
                passed[i] = copies.start(spot, spot, mate)
                total = add(total, sums_of(origin + core))
            for i in range(1, half):
                passed[i].wait_recv()
                origin = lax.rem(yy - i + half, half) * 2
                total = add(total, sums_of(origin + 1 - core))
            for k in range(above):
                flight[t, p, 1 + k].wait_recv()
                pend[t + 1 + k, p] = pend[t + 1 + k, p] + rx[t][n, 1 + k].astype(F32) - total[k]
                if t + 1 == mid:
                    hand_over(k, p)
            if t + 1 < mid:
                for q in own(t + 1):
                    if theirs(t + 1, q) == p:
                        offer_urgent(t + 1, q, pend[t + 1, p])
                        offer_rest(t + 1, q, [pend[s, p] for s in range(t + 2, levels)])

        def later_work(t=t, first_block=first_block):
            z_all = jnp.concatenate(
                [zs[t][n].reshape(n_row * rows, LANES) for n in range(counts[t])], axis=1
            )
            y_here = dot(anc[first_block], z_all).astype(BF)
            for other in range(n_row):
                acc[t][other] = tdot(anc[first_block, :, other * rows : (other + 1) * rows], y_here)

    for q in range(3, PIECES):
        spread_first(1, q)
    later_work()
    for k in range(supers):
        inv_t[k] = inv[k].T
    for q in range(PIECES // 2):
        spread_last(0, q)
    for q in range(PIECES // 2, PIECES):
        spread_last(0, q)
    for name in ("cross", "top", "mid"):
        loads[name].wait()
    halves.wait_recv()
    for q in range(3):
        spread_next(1, q)

    def gathered(j):
        for i in range(1, n_row):
            near[j, i].wait_recv()
        for i in range(n_row):
            far[j, i].wait_recv()
        return zr[0, j].astype(F32) + zr[1, j].astype(F32)

    cuts = [slice(0, half * rows), slice(half * rows, n_row * rows)]
    z_mid = gathered(0).astype(BF)
    zx[yy] = z_mid
    asked = [
        copies.start(zx.at[yy], zx.at[yy], {"row": lax.rem(yy + i, half) * 2 + core})
        for i in range(1, half)
    ]
    spread_done(0)
    product = dot_t(z_mid, full[0, cuts[0]])
    mixed = gathered(1)
    last = []
    for cut in cuts:
        if cut is not cuts[0]:
            product = dot_t(z_mid, full[0, cut])
        kt[:, cut] = mixed[:, cut] - product
        tt[:, cut] = kt[:, cut].astype(BF)
        last.append(copies.start(tt.at[:, cut], rt.at[:, cut], across[top]))
    for q in range(3, PIECES):
        spread_next(1, q)
    for q in range(PIECES // 2):
        spread_last(1, q)
    for copy in asked:
        copy.wait_recv()
    tall = n_row * rows
    yx[...] = dot_t(zx[...].reshape(half * strip, tall), pair[...]).astype(BF)
    pf[...] = dot(yx[...], pair[...]).reshape(half, strip, tall)
    px[...] = pf[...].astype(BF)
    told = []
    for i in range(1, half):
        other = lax.rem(yy + i, half)
        told.append(copies.start(px.at[other], qx.at[yy], {"row": other * 2 + core}))
    for q in range(PIECES // 2, PIECES):
        spread_last(1, q)
    spread_done(1)
    for side, copy in enumerate(last):
        copy.wait_recv()
        cut = cuts[side]
        tt2[:, cut] = (kt[:, cut] + rt[:, cut].astype(F32)).astype(BF)
        for r in range(side * half, (side + 1) * half):
            part = slice(r * rows, (r + 1) * rows)
            reach = slice(0, (r + 1) * rows)
            yt[:, part] = dot_t(tt2[:, reach], full[1, part, reach]).astype(BF)
    back = {}

    def give_back(j):
        here = pl.ds(pl.multiple_of(row * strip, strip), strip)
        sides = [peers, friends] if splits[mid] else [peers]
        for side, group in reversed(list(enumerate(sides))):
            for i in range(1 - side, n_row):
                part = st.at[j, :, slab(peers[i]["row"])]
                back[j, side, i] = copies.start(part, wr.at[j, side, here], group[i])
        wr[j, 0, here] = st[j, :, slab(row)]

    def take_back(j):
        for side, p in ((0, kept_block), (1, given_block)):
            if side == 0 or splits[mid]:
                for i in range(1 - side, n_row):
                    back[j, side, i].wait_recv()
                wide[mid + j, p] = wr[j, side].T

    for r in range(n_row):
        part = slice(r * rows, (r + 1) * rows)
        below = slice(r * rows, n_row * rows)
        st[1, :, part] = dot(yt[:, below], full[1, below, part]).astype(BF)
    give_back(1)
    value = pf[yy] - dot(st[1], full[0])
    for copy in told:
        copy.wait_recv()
    for i in range(1, half):
        value = value + qx[lax.rem(yy + i, half)].astype(F32)
    st[0] = value.astype(BF)
    give_back(0)
    arriving = {}

    def need(s, p):
        copy = arriving.pop((s, p), None)
        if copy is not None:
            copy.wait_recv()

    def widen(s, p, t):
        if splits[t]:
            arriving[s, p - counts[t]] = copies.start(
                wide.at[s, p], wide.at[s, p - counts[t]], across[t]
            )

    def leaf_back(first, last, p):
        terms = jnp.concatenate([wide[s, p] for s in range(first, last)], axis=0)
        return ly[:, columns[p]] - dot(mk[:, first * rows : last * rows], terms)

    for j in (1, 0):
        take_back(j)
        for p in own(mid - 1):
            widen(mid + j, p, mid - 1)

    ring = list(range(1, half)) + [0]
    for t in reversed(range(mid)):
        first_block = block_start(t, levels)
        second, kept, first = {}, {}, {}

        def part_of(dest, p):
            cut = pl.ds(pl.multiple_of(dest * rows, LANES), rows)
            n = p - (blocks - counts[t])
            value = acc[t][dest, :, n * LANES : (n + 1) * LANES]
            for s in range(t + 1, levels):
                value = value - dot(atr[first_block + s - t, cut], wide[s, p])
            return value

        for p in reversed(own(t)):
            n = p - (blocks - counts[t])
            for s in range(t + 1, levels):
                need(s, p)
            for i in ring:
                dest = lax.rem(yy + i, half) * 2 + 1 - core
                ps[t][n, i] = part_of(dest, p).astype(BF)
                first[p, i] = copies.start(ps[t].at[n, i], pr[t].at[n, i], mate)
        for p in reversed(own(t)):
            n = p - (blocks - counts[t])
            for i in ring[:-1]:
                dest = lax.rem(yy + i, half) * 2 + core
                value = part_of(dest, p)
                first[p, i].wait_recv()
                qs[t][n, i - 1] = (value + pr[t][n, i].astype(F32)).astype(BF)
                second[p, i] = copies.start(
                    qs[t].at[n, i - 1], qr[t].at[n, i - 1], {"row": dest}
                )
        for p in reversed(own(t)):
            n = p - (blocks - counts[t])
            for s in range(t + 1, levels if t + 1 < mid else mid):
                widen(s, p, t)
            value = part_of(row, p)
            first[p, 0].wait_recv()
            kept[p] = value + pr[t][n, 0].astype(F32)
        if t == 0:
            for p in reversed(own(t)[1:]):
                ly[:, columns[p]] = leaf_back(1, levels, p)
        for p in reversed(own(t)):
            n = p - (blocks - counts[t])
            value = kept[p]
            for i in ring[:-1]:
                second[p, i].wait_recv()
                value = value + qr[t][n, i - 1].astype(F32)
            wide[t, p] = value.astype(BF)
            widen(t, p, t)
            if t == 0 and levels > 1 and p == own(t)[-1]:
                ly[:, columns[own(t)[0]]] = leaf_back(1, levels, own(t)[0])
    for p in reversed(own(0)):
        leaf_out[:, columns[p]] = leaf_back(0, 1, p).astype(BF)
    for p in reversed(range(blocks - counts[0])):
        for s in range(1, levels):
            need(s, p)
        if levels > 1:
            ly[:, columns[p]] = leaf_back(1, levels, p)
    for s in range(levels):
        for p in own(0):
            out[s * rows : (s + 1) * rows, columns[p]] = wide[s, p]
    for p in reversed(range(blocks - counts[0])):
        need(0, p)
        leaf_out[:, columns[p]] = leaf_back(0, 1, p).astype(BF)
        for s in range(levels):
            out[s * rows : (s + 1) * rows, columns[p]] = wide[s, p]
    for copy in copies.all:
        copy.wait_send()


def solve(leaf_rhs, leaf_inv, coupling, pattern, anc_rhs, anc):
    levels, rows, cols = anc_rhs.shape
    leaf_rows = leaf_rhs.shape[0]
    supers, width = leaf_inv.shape[:2]
    n_row = lax.axis_size("row")
    half = n_row // 2
    blocks = cols // LANES
    counts, splits = plan(levels, cols)
    span = range(levels - 2)
    early = block_start(levels - 2, levels)
    strip, tall = LANES // n_row, n_row * rows
    less = max(half - 1, 1)
    scratch = [
        pltpu.VMEM(leaf_rhs.shape, BF),
        pltpu.VMEM(leaf_inv.shape, BF),
        pltpu.VMEM(coupling.shape, BF),
        pltpu.VMEM(anc_rhs.shape, F32),
        pltpu.VMEM((early,) + anc.shape[1:], BF),
        pltpu.VMEM((leaf_rows, cols), F32),
        pltpu.VMEM((leaf_rows, cols), BF),
        pltpu.VMEM((leaf_rows, levels * rows), BF),
        pltpu.VMEM((levels, rows, leaf_rows), BF),
        pltpu.VMEM((early, n_row * rows, rows), BF),
        pltpu.VMEM((levels, blocks, rows, LANES), F32),
        pltpu.VMEM((levels, blocks, rows, LANES), BF),
    ]
    scratch += [
        pltpu.VMEM((2, tall, tall), BF),
        pltpu.VMEM((2 * rows, tall), BF),
        pltpu.VMEM((2, 2, LANES, rows), BF),
        pltpu.VMEM((2, 2, strip, tall), BF),
        pltpu.VMEM((strip, tall), F32),
        pltpu.VMEM((strip, tall), BF),
        pltpu.VMEM((strip, tall), BF),
        pltpu.VMEM((2, strip, tall), BF),
        pltpu.VMEM((2, 2, LANES, rows), BF),
        pltpu.VMEM((half, strip, tall), BF),
        pltpu.VMEM((half * strip, 2 * rows), BF),
        pltpu.VMEM((half, strip, tall), F32),
        pltpu.VMEM((half, strip, tall), BF),
        pltpu.VMEM((half, strip, tall), BF),
        pltpu.VMEM((strip, tall), BF),
        pltpu.VMEM((strip, tall), BF),
    ]
    scratch += [pltpu.VMEM((counts[t], levels - t, rows, LANES), BF) for t in span]
    scratch += [pltpu.VMEM((counts[t], levels - t, rows, LANES), BF) for t in span]
    scratch += [pltpu.VMEM((counts[t], n_row, rows, LANES), BF) for t in span]
    scratch += [pltpu.VMEM((n_row, rows, counts[t] * LANES), F32) for t in span]
    scratch += [pltpu.VMEM((counts[t], half, rows, LANES), BF) for t in span]
    scratch += [pltpu.VMEM((counts[t], half, rows, LANES), BF) for t in span]
    scratch += [pltpu.VMEM((counts[t], less, rows, LANES), BF) for t in span]
    scratch += [pltpu.VMEM((counts[t], less, rows, LANES), BF) for t in span]
    total = copies_needed(levels, n_row, counts)
    scratch += [pltpu.SemaphoreType.DMA((total,)), pltpu.SemaphoreType.DMA((total,))]
    scratch += [pltpu.SemaphoreType.DMA((2 * levels + 6,))]
    away = pl.BlockSpec(memory_space=pl.ANY)
    return pl.pallas_call(
        functools.partial(kernel, (levels, n_row, blocks, supers, width)),
        out_shape=(
            pltpu.VMEM((leaf_rows, cols), BF),
            pltpu.VMEM((levels * rows, cols), BF),
            pltpu.VMEM(leaf_inv.shape, BF),
        ),
        in_specs=[away, away, away, pl.BlockSpec(memory_space=pltpu.SMEM), away, away],
        out_specs=(pl.BlockSpec(memory_space=pltpu.VMEM),) * 3,
        scratch_shapes=scratch,
        compiler_params=pltpu.CompilerParams(collective_id=0, has_side_effects=True, vmem_limit_bytes=VMEM_BYTES),
        name="solve",
    )(leaf_rhs, leaf_inv, coupling, pattern, anc_rhs, anc)


def tail_kernel(inv_t, vb, solved, x_leaf, x_anc, leaf, anc, sems):
    count, width = inv_t.shape[:2]
    size = anc.shape[0] // PARTS
    copies = []

    def finish(src, dst, part):
        copy = pltpu.make_async_copy(src.at[part], dst.at[part], sems.at[len(copies)])
        copy.start()
        copies.append(copy)

    for k in range(PARTS):
        part = pl.ds(k * size, size)
        anc[part] = solved[part].astype(F32)
        finish(anc, x_anc, part)
    for k in range(count):
        part = pl.ds(k * width, width)
        leaf[part] = dot(inv_t[k], vb[part])
        finish(leaf, x_leaf, part)
    for copy in copies:
        copy.wait()


def tail(inv_t, leaf_vb, solved):
    count = inv_t.shape[0]
    result = (
        jax.ShapeDtypeStruct(leaf_vb.shape, F32),
        jax.ShapeDtypeStruct(solved.shape, F32),
    )
    return pl.pallas_call(
        tail_kernel,
        out_shape=result,
        in_specs=[pl.BlockSpec(memory_space=pltpu.VMEM)] * 3,
        out_specs=(pl.BlockSpec(memory_space=pl.ANY),) * 2,
        scratch_shapes=[
            pltpu.VMEM(leaf_vb.shape, F32),
            pltpu.VMEM(solved.shape, F32),
            pltpu.SemaphoreType.DMA((count + PARTS,)),
        ],
        name="tail",
    )(inv_t, leaf_vb, solved)


def body(leaf_rhs, leaf_inv, coupling, pattern, anc_rhs, anc_blocks):
    _, levels, rows, cols = anc_rhs.shape
    leaf_vb, solved, inv_t = solve(
        leaf_rhs, leaf_inv, coupling.transpose(1, 0, 2), pattern.T, anc_rhs[0], anc_blocks[0]
    )
    leaf_vb = pltpu.with_memory_space_constraint(leaf_vb, pltpu.VMEM)
    solved = pltpu.with_memory_space_constraint(solved, pltpu.VMEM)
    inv_t = pltpu.with_memory_space_constraint(inv_t, pltpu.VMEM)
    x_leaf, x_anc = tail(inv_t, leaf_vb, solved)
    return (x_leaf, x_anc.reshape(1, levels, rows, cols))


def solution(mesh):
    placed = (
        P(("layer", "row"), None),
        P(("layer", "row"), None, None),
        P(("layer", "row"), None, None),
        P(("layer", "row"), None),
        P("layer", None, "row", None),
        P("layer", None, "row", None),
    )
    return jax.shard_map(
        body,
        mesh=mesh,
        in_specs=placed,
        out_specs=(P(("layer", "row"), None), P("layer", None, "row", None)),
        check_vma=False,
    )
```
